256 devices in a mesh: sib: 2 (over core), row: 8 (over z), col: 16 (over x, y).
Axes of the slice: x: 4, y: 4, z: 8, core: 2. Of those that a mesh axis runs over, the one named last changes fastest.
Arguments:
- front_inverse: bfloat16 [24576, 24576], P('row', 'col'), may hold values from -0.078125 to 0.078125
- panel: bfloat16 [2, 12288, 256], P('sib', 'col'), may hold values from -0.59765625 to 0.59765625
- row_map: int32 [2, 12288], P('sib'), may hold values from 0 to 24575, as said below
- diag_inverse: float32 [2, 256, 256], P('sib'), may hold values from -6 to 6
Outputs:
- offdiag_block: float32 [2, 24576, 256], P('sib', ('row', 'col'))
- diag_block: float32 [2, 256, 256], P('sib')
The draws below stay inside these ranges and needn't reach their ends.
Inputs may be any that keep to these rules, and one draw needn't show every extreme that they name: Each row of row_map names 12288 different front rows in increasing order, the first 0 and the last 24575.
All inputs are finite; a program needn't handle non-finite values.
Results may differ from the reference program's by a relative error of at most 0.0003.
Values may be sent and summed in bfloat16 or wider, within the bound.
A program may use at most 64 MiB of HBM per device.

```python
import jax
import jax.numpy as jnp
from jax import lax

F = 24576
W = 256
R = 12288


def chosen_rows(key, which):
    base = jax.random.fold_in(key, 71 + which)
    block = F // 16
    levels = jnp.array([4, 4, 4, 4, 4, 2, 2, 2, 2, 1, 1, 1, 1, 0, 0, 0], jnp.int32)
    counts = jax.random.permutation(jax.random.fold_in(base, 5), levels) * (block // 4)
    block_keys = jax.random.split(jax.random.fold_in(base, 9), 16)
    ranks = jax.vmap(lambda k: jax.random.permutation(k, block))(block_keys)
    picked = (ranks < counts[:, None]).reshape(F)
    index = jnp.arange(F, dtype=jnp.int32)
    order_keys = jnp.where(picked, index, index + F).astype(jnp.int32)
    ordered = jnp.argsort(order_keys, stable=True).astype(jnp.int32)
    rows = ordered[:R]
    rows = rows.at[0].set(0)
    rows = rows.at[R - 1].set(F - 1)
    return rows.astype(jnp.int32)


def draw_row_map(key, part):
    return jnp.stack([chosen_rows(key, 0), chosen_rows(key, 1)]).astype(jnp.int32)


def spiked(drawn, stream_key, source, target, blocks, factor):
    def block_of(axis_at):
        return (jnp.arange(drawn.shape[axis_at]) // (drawn.shape[axis_at] // blocks)).reshape((-1,) + (1,) * (drawn.ndim - 1 - axis_at))

    first = jax.random.permutation(stream_key, blocks)[block_of(target)]
    second = (block_of(target) + blocks // 2) % blocks
    return jnp.where((block_of(source) == first) | (block_of(source) == second), factor * drawn, drawn)


def steps_of(rng, dims, shards, least, largest):
    factor_of, own = 1.0, jax.random.fold_in(rng, 6)
    for dim, blocks in shards:
        heights = jnp.exp(jax.random.uniform(jax.random.fold_in(own, dim), (blocks,), jnp.float32, least / len(shards), largest / len(shards)))
        factor_of = factor_of * jnp.repeat(heights, dims[dim] // blocks).reshape([-1 if axis == dim else 1 for axis in range(len(dims))])
    return factor_of


def scatter_about(stream_key, shape, scale, bound, cuts=(), kind=jnp.bfloat16):
    loudness = steps_of(stream_key, shape, cuts, -0.22, 0.18) if cuts else 1.0
    entries = jax.random.normal(stream_key, shape, jnp.float32) * scale * loudness
    return jnp.minimum(jnp.maximum(entries, -bound), bound).astype(kind)


def noise_with(own_key, shape, width, most, pieces, heavy, kind=jnp.bfloat16):
    values = width * jax.random.normal(own_key, shape, jnp.float32)
    if pieces:
        values = values * steps_of(own_key, shape, pieces, -0.22, 0.18)
    return jnp.clip(spiked(values, jax.random.fold_in(own_key, 3), *heavy), -most, most).astype(kind)


def setup_inputs(seed: int = 0) -> dict:
    key_of = jax.random.split(jax.random.key(seed), 5)
    front_inverse = noise_with(key_of[0], (F, F), R ** -0.5, 0.078125, ((0, 8), (1, 16)), (1, 0, 16, 2.0))
    panel = scatter_about(key_of[1], (2, R, W), 0.1, 0.59765625, ((0, 2), (1, 16)))
    row_map = draw_row_map(jax.random.fold_in(key_of[4], 71), 0)
    diag_inverse = scatter_about(key_of[3], (2, W, W), 1.0, 6.0, ((0, 2),), jnp.float32)
    return {"front_inverse": front_inverse, "panel": panel, "row_map": row_map, "diag_inverse": diag_inverse}


def one_panel(front_inverse, rows, places, diag_part):
    spread = jnp.zeros((F, W), jnp.bfloat16).at[places].set(rows)
    product = jnp.dot(front_inverse, spread, preferred_element_type=jnp.float32)
    marks = jnp.zeros((F,), jnp.float32).at[places].set(1.0)
    offdiag = jnp.where(marks[:, None] > 0.5, -product, jnp.zeros_like(product))
    diag = diag_part + jnp.dot(spread.astype(jnp.float32).T, product, precision=lax.Precision.HIGHEST)
    return offdiag, diag


def reference(front_inverse, panel, row_map, diag_inverse):
    first_off, first_diag = one_panel(front_inverse, panel[0], row_map[0], diag_inverse[0])
    second_off, second_diag = one_panel(front_inverse, panel[1], row_map[1], diag_inverse[1])
    return (jnp.stack([first_off, second_off]), jnp.stack([first_diag, second_diag]))
```

```python
import functools

import jax
import jax.numpy as jnp
from jax import lax
from jax.experimental import pallas as pl
from jax.experimental.pallas import tpu as pltpu
from jax.sharding import Mesh
from jax.sharding import PartitionSpec as P

COL = ("col_0", "col_1")
ROW_COL = ("row", "col_0", "col_1")
MESH_ID = pl.DeviceIdType.MESH
LANES = 128
GROUP = 16
SIDE = 4
SPAN = 8
F32 = jnp.float32
BF16 = jnp.bfloat16


def kernel(
    panel, places, front, dinv, off_out, diag_out,
    gath, wind, spread, front_v, part, ring_1, mid, ring_2, own_s, hits,
    terms, got_d, sum_z, got_z, total,
    send, rg, rz, r1, r2, rs, rd, rzz, rt, loc,
):
    nblk = panel.shape[0]
    nchunk = places.shape[0]
    front_rows, front_cols = front.shape
    ntgt = front_cols // LANES
    nwin = wind.shape[1]
    own = own_s.shape[0]
    z = lax.axis_index("row")
    pos = {"col_0": lax.axis_index("col_0"), "col_1": lax.axis_index("col_1")}
    px, py = pos["col_0"], pos["col_1"]
    col = px * SIDE + py
    order = (("col_0", "col_1"), ("col_1", "col_0"))
    sends = []

    def put(src, dst, sem, **device):
        copy = pltpu.make_async_remote_copy(
            src_ref=src, dst_ref=dst, send_sem=send.at[len(sends)], recv_sem=sem,
            device_id=device, device_id_type=MESH_ID,
        )
        copy.start()
        sends.append(copy)

    def arrive(dst, sem):
        pltpu.make_async_copy(dst, dst, sem).wait()

    def step(axis, delta):
        return {axis: lax.rem(pos[axis] + delta + SIDE, SIDE)}

    def in_plane(off):
        peer = lax.rem(col + off, SIDE * SIDE)
        return peer, {"col_0": peer // SIDE, "col_1": lax.rem(peer, SIDE)}

    to_row = col // 2
    to_col = SPAN * lax.rem(col, 2) + z
    from_col = 2 * z + col // SPAN
    from_row = lax.rem(col, SPAN)
    stays = jnp.logical_and(to_row == z, to_col == col)
    goes = jnp.logical_not(stays)
    to_dev = {"row": to_row, "col_0": to_col // SIDE, "col_1": lax.rem(to_col, SIDE)}
    from_dev = {"row": from_row, "col_0": from_col // SIDE, "col_1": lax.rem(from_col, SIDE)}

    load_front = pltpu.make_async_copy(front, front_v, loc.at[0])
    load_front.start()

    barrier = pltpu.get_barrier_semaphore()
    for off in range(1, SIDE * SIDE):
        pl.semaphore_signal(barrier, inc=1, device_id=in_plane(off)[1], device_id_type=MESH_ID)
    for off in range(1, SPAN):
        pl.semaphore_signal(
            barrier, inc=1, device_id={"row": lax.rem(z + off, SPAN)}, device_id_type=MESH_ID
        )

    @pl.when(goes)
    def _():
        pl.semaphore_signal(barrier, inc=1, device_id=to_dev, device_id_type=MESH_ID)
        pl.semaphore_signal(barrier, inc=1, device_id=from_dev, device_id_type=MESH_ID)

    pl.semaphore_wait(barrier, SIDE * SIDE - 1 + SPAN - 1 + 2 * goes.astype(jnp.int32))

    def slot(h, d0, d1):
        a0, a1 = order[h]
        c0 = lax.rem(pos[a0] + d0, SIDE)
        c1 = lax.rem(pos[a1] + d1, SIDE)
        k = c0 * SIDE + c1 if h == 0 else c1 * SIDE + c0
        return gath.at[h, pl.ds(k * nblk, nblk)]

    def mine(h):
        return panel.at[:, z, :, pl.ds(h * LANES, LANES)]

    def pass_on(h, d0, d1, which, delta, src=None):
        dst = slot(h, d0, d1)
        d0, d1 = ((d0 - delta) % SIDE, d1) if which == 0 else (d0, (d1 - delta) % SIDE)
        put(dst if src is None else src, dst, rg.at[h, d0, d1], **step(order[h][which], delta))

    def gathered(h, d0, d1):
        arrive(slot(h, d0, d1), rg.at[h, d0, d1])

    for h in range(2):
        for delta in (1, -1, 2):
            pass_on(h, 0, 0, 0, delta, mine(h))
        for delta in (1, -1):
            pass_on(h, 0, 0, 1, delta, mine(h))
    keep = [pltpu.make_async_copy(mine(h), slot(h, 0, 0), loc.at[1 + h]) for h in range(2)]
    for copy in keep:
        copy.start()

    place = places[...]

    def chunk_of(bound):
        return jnp.sum((place < bound).astype(jnp.int32)) // LANES

    col_base = col * front_cols
    chunks = [chunk_of(col_base + t * LANES) for t in range(ntgt)]
    first = jnp.minimum(chunks[0], nchunk - nwin)
    own_base = z * front_rows + col * own
    nown = hits.shape[0]
    own_first = jnp.minimum(chunk_of(own_base), nchunk - nown)
    target = lax.broadcasted_iota(jnp.int32, (own, LANES), 0) + own_base
    mark = jnp.zeros((own, LANES), F32)
    for i in range(nown):
        mark += jnp.where(places[pl.ds(own_first + i, 1), :] == target, 1.0, 0.0)
    hit_rows = jnp.broadcast_to(jnp.max(mark, axis=1, keepdims=True), (own, LANES))
    hits[0] = hit_rows

    for d in (1, 3):
        for h in range(2):
            gathered(h, d, 0)
            pass_on(h, d, 0, 1, 1)
            pass_on(h, d, 0, 1, -1)
    for h in range(2):
        gathered(h, 0, 3)
        pass_on(h, 0, 3, 1, 1)
    for h in range(2):
        gathered(h, 2, 0)
        pass_on(h, 2, 0, 1, 1)
        pass_on(h, 2, 0, 1, -1)
    for h in range(2):
        gathered(h, 1, 3)
        pass_on(h, 1, 3, 1, 1)
        gathered(h, 3, 1)
        pass_on(h, 3, 1, 1, -1)
    for h in range(2):
        gathered(h, 2, 1)
        pass_on(h, 2, 1, 1, -1)
    for copy in keep:
        copy.wait()
    for h in range(2):
        for d in ((0, 1), (2, 3), (3, 3), (1, 1), (0, 2), (1, 2), (2, 2), (3, 2)):
            gathered(h, *d)

    for h in range(2):
        for i in range(nwin):
            wind[h, i, z] = gath[h, first + i]

    def share(h, d):
        return wind.at[h, :, lax.rem(z + d + SPAN, SPAN)]

    last = ((SPAN // 2, SPAN // 2 - 1), (SPAN // 2 - 1, SPAN // 2))
    for s in range(1, SPAN // 2 + 1):
        for h in range(2):
            for d, sign in enumerate((1, -1)):
                if s <= last[h][d]:
                    if s > 1:
                        arrive(share(h, -sign * (s - 1)), rz.at[h, d, s - 2])
                    block = share(h, -sign * (s - 1))
                    put(block, block, rz.at[h, d, s - 1], row=lax.rem(z + sign + SPAN, SPAN))
    for h in range(2):
        for d, sign in enumerate((1, -1)):
            arrive(share(h, -sign * last[h][d]), rz.at[h, d, last[h][d] - 1])

    rows_at = lax.broadcasted_iota(jnp.int32, (LANES, LANES), 0)
    for t in range(ntgt):
        a = jnp.minimum(chunks[t] - first, nwin - 2)
        want = rows_at + (col_base + t * LANES)
        table = jnp.concatenate(
            [
                jnp.where(places[pl.ds(first + a + i, 1), :] == want, 1.0, 0.0).astype(BF16)
                for i in range(2)
            ],
            axis=1,
        )
        for h in range(2):
            rows = wind[h, pl.ds(a, 2)].reshape(2 * LANES, LANES)
            spread[pl.ds(t * LANES, LANES), pl.ds(h * LANES, LANES)] = jnp.dot(
                table, rows, preferred_element_type=F32
            ).astype(BF16)

    given = spread.at[pl.ds(pl.multiple_of(z * own, GROUP), own)]
    give = pltpu.make_async_remote_copy(
        src_ref=given, dst_ref=own_s, send_sem=loc.at[3], recv_sem=rs,
        device_id=to_dev, device_id_type=MESH_ID,
    )

    @pl.when(goes)
    def _():
        give.start()

    @pl.when(stays)
    def _():
        copy = pltpu.make_async_copy(given, own_s, loc.at[4])
        copy.start()
        copy.wait()

    def near(h, d, j, src=None):
        put(part.at[h, 1 if d == 0 else 3, j], ring_1.at[h, d, j], r1.at[h, d, j],
            **step(order[h][0], 1 - 2 * d))

    def far(h, d, j):
        at = SIDE + j % 2
        put(part.at[h, 2, j], ring_1.at[h, d, at], r1.at[h, d, at], **step(order[h][0], 1 - 2 * d))

    load_front.wait()
    stripe = SIDE * own
    for d in (2, 1, 3, 0):
        at = pl.multiple_of(lax.rem(px + d, SIDE) * stripe, stripe)
        block = jnp.dot(
            front_v[pl.ds(at, stripe), :], spread[...], preferred_element_type=F32
        )
        for y in range(SIDE):
            j = lax.rem(y - py + SIDE, SIDE)
            part[0, d, j] = block[y * own:(y + 1) * own, :LANES]
            part[1, j, d] = block[y * own:(y + 1) * own, LANES:]
        if d == 2:
            for j in range(SIDE):
                far(0, j // 2, j)
        if d == 1:
            near(0, 0, 2)
            near(0, 0, 3)
        if d == 3:
            near(0, 1, 0)
            near(0, 1, 1)
        far(1, d // 2, d)
        near(1, 0 if d >= 2 else 1, d)
    for jj in range(2):
        for h in range(2):
            for d in range(2):
                j = 2 * d + jj
                arrive(ring_1.at[h, d, SIDE + jj], r1.at[h, d, SIDE + jj])
                at = 1 if d == 0 else 3
                part[h, at, j] = part[h, at, j] + ring_1[h, d, SIDE + jj]
                near(h, d, j)

    half = own // 2

    def near_2(h, d, u):
        put(mid.at[h, 1 if d == 0 else 3, u], ring_2.at[h, d, u], r2.at[h, d, u],
            **step(order[h][1], 1 - 2 * d))

    for j in (2, 1, 3, 0):
        for h in range(2):
            for d in range(2):
                arrive(ring_1.at[h, d, j], r1.at[h, d, j])
            both = part[h, 0, j] + ring_1[h, 0, j] + ring_1[h, 1, j]
            mid[h, j, 0] = both[:half]
            mid[h, j, 1] = both[half:]
            if j == 2:
                for d in range(2):
                    put(mid.at[h, 2, d], ring_2.at[h, d, 2], r2.at[h, d, 2],
                        **step(order[h][1], 1 - 2 * d))
            if j == 1:
                near_2(h, 0, 1)
            if j == 3:
                near_2(h, 1, 0)
    for h in range(2):
        for d in range(2):
            arrive(ring_2.at[h, d, 2], r2.at[h, d, 2])
            at = 1 if d == 0 else 3
            mid[h, at, d] = mid[h, at, d] + ring_2[h, d, 2]
            near_2(h, d, d)
    halves = []
    for h in range(2):
        both = []
        for u in range(2):
            for d in range(2):
                arrive(ring_2.at[h, d, u], r2.at[h, d, u])
            both.append(mid[h, 0, u] + ring_2[h, 0, u] + ring_2[h, 1, u])
        halves.append(jnp.concatenate(both, axis=0))
    hit_rows = hits[0]
    for h in range(2):
        off_out[:, pl.ds(h * LANES, LANES)] = jnp.where(hit_rows > 0.5, -halves[h], 0.0)
    product = jnp.concatenate(halves, axis=1)

    @pl.when(goes)
    def _():
        give.wait()

    high = product.astype(BF16)
    low = (product - high.astype(F32)).astype(BF16)
    rows = own_s[...]
    dims = (((0,), (0,)), ((), ()))
    here = lax.dot_general(rows, high, dims, preferred_element_type=F32)
    here += lax.dot_general(rows, low, dims, preferred_element_type=F32)
    terms[...] = here.reshape(terms.shape)
    for off in range(1, SIDE * SIDE):
        peer, device = in_plane(off)
        put(terms.at[peer], got_d.at[off - 1], rd.at[off - 1], **device)
    acc = terms[col]
    for off in range(1, SIDE * SIDE):
        arrive(got_d.at[off - 1], rd.at[off - 1])
        acc += got_d[off - 1]
    sum_z[...] = acc
    for off in range(1, SPAN):
        put(sum_z, got_z.at[off - 1], rzz.at[off - 1], row=lax.rem(z + off, SPAN))
    for off in range(1, SPAN):
        arrive(got_z.at[off - 1], rzz.at[off - 1])
    acc = jnp.zeros_like(acc)
    got_z[SPAN - 1] = sum_z[...]
    for r in range(SPAN):
        at = lax.rem(z - r + SPAN - 1 + SPAN, SPAN)
        acc += got_z[at]
    total[col] = acc
    for off in range(1, SIDE * SIDE):
        peer, device = in_plane(off)
        put(total.at[col], total.at[col], rt.at[off - 1], **device)
    for off in range(1, SIDE * SIDE):
        peer = lax.rem(col - off + SIDE * SIDE, SIDE * SIDE)
        arrive(total.at[peer], rt.at[off - 1])
    diag_out[...] = dinv[...] + total[...].reshape(dinv.shape)
    for copy in sends:
        copy.wait_send()


def shards(front_inverse, panel, row_map, diag_inverse):
    front_rows, front_cols = front_inverse.shape
    _, block, width = panel.shape
    count = row_map.shape[1]
    nchunk = count // LANES
    nwin = front_cols // LANES + 1
    own = front_rows // (SIDE * SIDE)
    nown = (own + 2 * LANES - 2) // LANES
    slab = width // (SIDE * SIDE)
    vmem = pltpu.VMEM
    dma = pltpu.SemaphoreType.DMA
    offdiag, diag = pl.pallas_call(
        kernel,
        out_shape=(
            jax.ShapeDtypeStruct((own, width), F32),
            jax.ShapeDtypeStruct((width, width), F32),
        ),
        in_specs=[
            pl.BlockSpec(memory_space=pl.ANY),
            pl.BlockSpec(memory_space=pltpu.VMEM),
            pl.BlockSpec(memory_space=pl.ANY),
            pl.BlockSpec(memory_space=pltpu.VMEM),
        ],
        out_specs=(
            pl.BlockSpec(memory_space=pltpu.VMEM),
            pl.BlockSpec(memory_space=pltpu.VMEM),
        ),
        scratch_shapes=[
            vmem((2, nchunk, GROUP, LANES), BF16),
            vmem((2, nwin, SPAN, GROUP, LANES), BF16),
            vmem((front_cols, width), BF16),
            vmem((front_rows, front_cols), BF16),
            vmem((2, SIDE, SIDE, own, LANES), F32),
            vmem((2, 2, SIDE + 2, own, LANES), F32),
            vmem((2, SIDE, 2, own // 2, LANES), F32),
            vmem((2, 2, 3, own // 2, LANES), F32),
            vmem((own, width), BF16),
            vmem((nown, own, LANES), F32),
            vmem((SIDE * SIDE, slab, width), F32),
            vmem((SIDE * SIDE - 1, slab, width), F32),
            vmem((slab, width), F32),
            vmem((SPAN, slab, width), F32),
            vmem((SIDE * SIDE, slab, width), F32),
            dma((160,)),
            dma((2, SIDE, SIDE)),
            dma((2, 2, SPAN // 2)),
            dma((2, 2, SIDE + 2)),
            dma((2, 2, 3)),
            dma,
            dma((SIDE * SIDE - 1,)),
            dma((SPAN - 1,)),
            dma((SIDE * SIDE - 1,)),
            dma((5,)),
        ],
        compiler_params=pltpu.CompilerParams(
            collective_id=0, has_side_effects=True, vmem_limit_bytes=60 * 1024 * 1024
        ),
        name="selected_inverse",
    )(
        panel.reshape(block // (SPAN * GROUP), SPAN, GROUP, width),
        row_map.reshape(nchunk, LANES),
        front_inverse,
        diag_inverse[0],
    )
    return offdiag[None], diag[None]


def solution(mesh):
    finer = Mesh(
        mesh.devices.reshape(mesh.shape["sib"], mesh.shape["row"], SIDE, SIDE),
        ("sib", "row", "col_0", "col_1"),
    )
    return jax.shard_map(
        shards,
        mesh=finer,
        in_specs=(P("row", COL), P("sib", COL, None), P("sib", None), P("sib", None, None)),
        out_specs=(P("sib", ROW_COL, None), P("sib", None, None)),
        check_vma=False,
    )
```

```python
import functools

import jax
import jax.numpy as jnp
from jax import lax
from jax.experimental import pallas as pl
from jax.experimental.pallas import tpu as pltpu
from jax.sharding import Mesh
from jax.sharding import PartitionSpec as P

COL = ("col_0", "col_1")
ROW_COL = ("row", "col_0", "col_1")
MESH_ID = pl.DeviceIdType.MESH
LANES = 128
GROUP = 16
LEVELS = 32767.0
TINY = 1e-33
SIDE = 4
SPAN = 8
F32 = jnp.float32
BF16 = jnp.bfloat16


def kernel(
    panel, places, front, dinv, off_out, diag_out,
    gath, wind, spread, front_v, part, out_1, ring_1, mid, out_2, ring_2, scale, own_s, hits,
    terms, got_d, sum_z, got_z, total,
    send, rg, rz, r1, r2, rs, rd, rzz, rt, loc,
):
    nblk = panel.shape[0]
    nchunk = places.shape[0]
    front_rows, front_cols = front.shape
    ntgt = front_cols // LANES
    nwin = wind.shape[1]
    own = own_s.shape[0]
    z = lax.axis_index("row")
    pos = {"col_0": lax.axis_index("col_0"), "col_1": lax.axis_index("col_1")}
    px, py = pos["col_0"], pos["col_1"]
    col = px * SIDE + py
    order = (("col_0", "col_1"), ("col_1", "col_0"))
    sends = []

    def put(src, dst, sem, **device):
        copy = pltpu.make_async_remote_copy(
            src_ref=src, dst_ref=dst, send_sem=send.at[len(sends)], recv_sem=sem,
            device_id=device, device_id_type=MESH_ID,
        )
        copy.start()
        sends.append(copy)

    def arrive(dst, sem):
        pltpu.make_async_copy(dst, dst, sem).wait()

    def step(axis, delta):
        return {axis: lax.rem(pos[axis] + delta + SIDE, SIDE)}

    def in_plane(off):
        peer = lax.rem(col + off, SIDE * SIDE)
        return peer, {"col_0": peer // SIDE, "col_1": lax.rem(peer, SIDE)}

    to_row = col // 2
    to_col = SPAN * lax.rem(col, 2) + z
    from_col = 2 * z + col // SPAN
    from_row = lax.rem(col, SPAN)
    stays = jnp.logical_and(to_row == z, to_col == col)
    goes = jnp.logical_not(stays)
    to_dev = {"row": to_row, "col_0": to_col // SIDE, "col_1": lax.rem(to_col, SIDE)}
    from_dev = {"row": from_row, "col_0": from_col // SIDE, "col_1": lax.rem(from_col, SIDE)}

    load_front = pltpu.make_async_copy(front, front_v, loc.at[0])
    load_front.start()

    barrier = pltpu.get_barrier_semaphore()
    for axis in ("col_0", "col_1"):
        for delta in (1, -1, 2):
            pl.semaphore_signal(
                barrier, inc=1, device_id=step(axis, delta), device_id_type=MESH_ID
            )
    for delta in (1, -1):
        pl.semaphore_signal(
            barrier, inc=1, device_id={"row": lax.rem(z + delta + SPAN, SPAN)},
            device_id_type=MESH_ID,
        )
    pl.semaphore_wait(barrier, 2 * (SIDE - 1) + 2)

    def slot(h, d0, d1):
        a0, a1 = order[h]
        c0 = lax.rem(pos[a0] + d0, SIDE)
        c1 = lax.rem(pos[a1] + d1, SIDE)
        k = c0 * SIDE + c1 if h == 0 else c1 * SIDE + c0
        return gath.at[h, pl.ds(k * nblk, nblk)]

    def mine(h):
        return panel.at[:, z, :, pl.ds(h * LANES, LANES)]

    def pass_on(h, d0, d1, which, delta, src=None):
        dst = slot(h, d0, d1)
        d0, d1 = ((d0 - delta) % SIDE, d1) if which == 0 else (d0, (d1 - delta) % SIDE)
        put(dst if src is None else src, dst, rg.at[h, d0, d1], **step(order[h][which], delta))

    def gathered(h, d0, d1):
        arrive(slot(h, d0, d1), rg.at[h, d0, d1])

    for h in range(2):
        for delta in (1, -1, 2):
            pass_on(h, 0, 0, 0, delta, mine(h))
        for delta in (1, -1):
            pass_on(h, 0, 0, 1, delta, mine(h))
    keep = [pltpu.make_async_copy(mine(h), slot(h, 0, 0), loc.at[1 + h]) for h in range(2)]
    for copy in keep:
        copy.start()

    place = places[...]

    def chunk_of(bound):
        return jnp.sum((place < bound).astype(jnp.int32)) // LANES

    col_base = col * front_cols
    chunks = [chunk_of(col_base + t * LANES) for t in range(ntgt)]
    first = jnp.minimum(chunks[0], nchunk - nwin)
    own_base = z * front_rows + col * own
    nown = hits.shape[0]
    own_first = jnp.minimum(chunk_of(own_base), nchunk - nown)
    target = lax.broadcasted_iota(jnp.int32, (own, LANES), 0) + own_base
    mark = jnp.zeros((own, LANES), F32)
    for i in range(nown):
        mark += jnp.where(places[pl.ds(own_first + i, 1), :] == target, 1.0, 0.0)
    hit_rows = jnp.broadcast_to(jnp.max(mark, axis=1, keepdims=True), (own, LANES))
    hits[0] = hit_rows

    for d in (1, 3):
        for h in range(2):
            gathered(h, d, 0)
            pass_on(h, d, 0, 1, 1)
            pass_on(h, d, 0, 1, -1)
    for h in range(2):
        gathered(h, 0, 3)
        pass_on(h, 0, 3, 1, 1)
    for h in range(2):
        gathered(h, 2, 0)
        pass_on(h, 2, 0, 1, 1)
        pass_on(h, 2, 0, 1, -1)
    for h in range(2):
        gathered(h, 1, 3)
        pass_on(h, 1, 3, 1, 1)
        gathered(h, 3, 1)
        pass_on(h, 3, 1, 1, -1)
    for h in range(2):
        gathered(h, 2, 1)
        pass_on(h, 2, 1, 1, -1)
    for copy in keep:
        copy.wait()
    for h in range(2):
        for d in ((0, 1), (2, 3), (3, 3), (1, 1), (0, 2), (1, 2), (2, 2), (3, 2)):
            gathered(h, *d)

    for h in range(2):
        for i in range(nwin):
            wind[h, i, z] = gath[h, first + i]

    def share(h, d):
        return wind.at[h, :, lax.rem(z + d + SPAN, SPAN)]

    last = ((SPAN // 2, SPAN // 2 - 1), (SPAN // 2 - 1, SPAN // 2))
    for s in range(1, SPAN // 2 + 1):
        for h in range(2):
            for d, sign in enumerate((1, -1)):
                if s <= last[h][d]:
                    if s > 1:
                        arrive(share(h, -sign * (s - 1)), rz.at[h, d, s - 2])
                    block = share(h, -sign * (s - 1))
                    put(block, block, rz.at[h, d, s - 1], row=lax.rem(z + sign + SPAN, SPAN))
    for h in range(2):
        for d, sign in enumerate((1, -1)):
            arrive(share(h, -sign * last[h][d]), rz.at[h, d, last[h][d] - 1])

    rows_at = lax.broadcasted_iota(jnp.int32, (LANES, LANES), 0)
    for t in range(ntgt):
        a = jnp.minimum(chunks[t] - first, nwin - 2)
        want = rows_at + (col_base + t * LANES)
        table = jnp.concatenate(
            [
                jnp.where(places[pl.ds(first + a + i, 1), :] == want, 1.0, 0.0).astype(BF16)
                for i in range(2)
            ],
            axis=1,
        )
        for h in range(2):
            rows = wind[h, pl.ds(a, 2)].reshape(2 * LANES, LANES)
            spread[pl.ds(t * LANES, LANES), pl.ds(h * LANES, LANES)] = jnp.dot(
                table, rows, preferred_element_type=F32
            ).astype(BF16)

    given = spread.at[pl.ds(pl.multiple_of(z * own, GROUP), own)]
    give = pltpu.make_async_remote_copy(
        src_ref=given, dst_ref=own_s, send_sem=loc.at[3], recv_sem=rs,
        device_id=to_dev, device_id_type=MESH_ID,
    )

    @pl.when(goes)
    def _():
        give.start()

    @pl.when(stays)
    def _():
        copy = pltpu.make_async_copy(given, own_s, loc.at[4])
        copy.start()
        copy.wait()

    def post(value, out, dst, at, sem, device):
        top = jnp.maximum(jnp.max(jnp.abs(value), axis=0, keepdims=True), TINY)
        out[...] = jnp.round(value * (LEVELS / top)).astype(jnp.int32).astype(jnp.int16)
        scale[(0, *at)] = top * (1.0 / LEVELS)
        put(scale.at[(0, *at)], scale.at[(1, *at)], sem.at[(1, *at[1:])], **device)
        put(out, dst, sem.at[(0, *at[1:])], **device)

    def fetch(dst, at, sem):
        arrive(scale.at[(1, *at)], sem.at[(1, *at[1:])])
        arrive(dst, sem.at[(0, *at[1:])])
        return dst[...].astype(jnp.int32).astype(F32) * scale[(1, *at)]

    def post_1(value, h, d, at):
        post(value, out_1.at[h, d, at], ring_1.at[h, d, at], (0, h, d, at), r1,
             step(order[h][0], 1 - 2 * d))

    def fetch_1(h, d, at):
        return fetch(ring_1.at[h, d, at], (0, h, d, at), r1)

    def near(h, d, j):
        post_1(part[h, 1 if d == 0 else 3, j], h, d, j)

    def far(h, d, j):
        post_1(part[h, 2, j], h, d, SIDE + j % 2)

    load_front.wait()
    stripe = SIDE * own
    for d in (2, 1, 3, 0):
        at = pl.multiple_of(lax.rem(px + d, SIDE) * stripe, stripe)
        block = jnp.dot(
            front_v[pl.ds(at, stripe), :], spread[...], preferred_element_type=F32
        )
        for y in range(SIDE):
            j = lax.rem(y - py + SIDE, SIDE)
            part[0, d, j] = block[y * own:(y + 1) * own, :LANES]
            part[1, j, d] = block[y * own:(y + 1) * own, LANES:]
        if d == 2:
            for j in range(SIDE):
                far(0, j // 2, j)
        if d == 1:
            near(0, 0, 2)
            near(0, 0, 3)
        if d == 3:
            near(0, 1, 0)
            near(0, 1, 1)
        far(1, d // 2, d)
        near(1, 0 if d >= 2 else 1, d)
    for jj in range(2):
        for h in range(2):
            for d in range(2):
                j = 2 * d + jj
                post_1(part[h, 1 if d == 0 else 3, j] + fetch_1(h, d, SIDE + jj), h, d, j)

    half = own // 2

    def post_2(value, h, d, at):
        post(value, out_2.at[h, d, at], ring_2.at[h, d, at], (1, h, d, at), r2,
             step(order[h][1], 1 - 2 * d))

    def fetch_2(h, d, at):
        return fetch(ring_2.at[h, d, at], (1, h, d, at), r2)

    for j in (2, 1, 3, 0):
        for h in range(2):
            both = part[h, 0, j] + fetch_1(h, 0, j) + fetch_1(h, 1, j)
            if j == 2:
                for d in range(2):
                    post_2(both[d * half:(d + 1) * half], h, d, 2)
            else:
                mid[h, j // 2 if j else 2] = both
            if j == 1:
                post_2(both[half:], h, 0, 1)
            if j == 3:
                post_2(both[:half], h, 1, 0)
    for h in range(2):
        for d in range(2):
            post_2(mid[h, d, pl.ds(d * half, half)] + fetch_2(h, d, 2), h, d, d)
    halves = []
    for h in range(2):
        both = []
        for u in range(2):
            rows = mid[h, 2, pl.ds(u * half, half)]
            both.append(rows + fetch_2(h, 0, u) + fetch_2(h, 1, u))
        halves.append(jnp.concatenate(both, axis=0))
    hit_rows = hits[0]
    for h in range(2):
        off_out[:, pl.ds(h * LANES, LANES)] = jnp.where(hit_rows > 0.5, -halves[h], 0.0)
    product = jnp.concatenate(halves, axis=1)

    @pl.when(goes)
    def _():
        give.wait()

    high = product.astype(BF16)
    low = (product - high.astype(F32)).astype(BF16)
    rows = own_s[...]
    dims = (((0,), (0,)), ((), ()))
    here = lax.dot_general(rows, high, dims, preferred_element_type=F32)
    here += lax.dot_general(rows, low, dims, preferred_element_type=F32)
    terms[...] = here.reshape(terms.shape)
    for off in range(1, SIDE * SIDE):
        peer, device = in_plane(off)
        put(terms.at[peer], got_d.at[off - 1], rd.at[off - 1], **device)
    acc = terms[col]
    for off in range(1, SIDE * SIDE):
        arrive(got_d.at[off - 1], rd.at[off - 1])
        acc += got_d[off - 1]
    sum_z[...] = acc
    for off in range(1, SPAN):
        put(sum_z, got_z.at[off - 1], rzz.at[off - 1], row=lax.rem(z + off, SPAN))
    for off in range(1, SPAN):
        arrive(got_z.at[off - 1], rzz.at[off - 1])
    acc = jnp.zeros_like(acc)
    got_z[SPAN - 1] = sum_z[...]
    for r in range(SPAN):
        at = lax.rem(z - r + SPAN - 1 + SPAN, SPAN)
        acc += got_z[at]
    total[col] = acc
    for off in range(1, SIDE * SIDE):
        peer, device = in_plane(off)
        put(total.at[col], total.at[col], rt.at[off - 1], **device)
    for off in range(1, SIDE * SIDE):
        peer = lax.rem(col - off + SIDE * SIDE, SIDE * SIDE)
        arrive(total.at[peer], rt.at[off - 1])
    diag_out[...] = dinv[...] + total[...].reshape(dinv.shape)
    for copy in sends:
        copy.wait_send()


def finish(off, diag, off_out, diag_out):
    off_out[...] = off[...]
    diag_out[...] = diag[...]


def shards(front_inverse, panel, row_map, diag_inverse):
    front_rows, front_cols = front_inverse.shape
    _, block, width = panel.shape
    count = row_map.shape[1]
    nchunk = count // LANES
    nwin = front_cols // LANES + 1
    own = front_rows // (SIDE * SIDE)
    nown = (own + 2 * LANES - 2) // LANES
    slab = width // (SIDE * SIDE)
    vmem = pltpu.VMEM
    dma = pltpu.SemaphoreType.DMA
    offdiag, diag = pl.pallas_call(
        kernel,
        out_shape=(
            jax.ShapeDtypeStruct((own, width), F32),
            jax.ShapeDtypeStruct((width, width), F32),
        ),
        in_specs=[
            pl.BlockSpec(memory_space=pl.ANY),
            pl.BlockSpec(memory_space=pltpu.VMEM),
            pl.BlockSpec(memory_space=pl.ANY),
            pl.BlockSpec(memory_space=pltpu.VMEM),
        ],
        out_specs=(
            pl.BlockSpec(memory_space=pltpu.VMEM),
            pl.BlockSpec(memory_space=pltpu.VMEM),
        ),
        scratch_shapes=[
            vmem((2, nchunk, GROUP, LANES), BF16),
            vmem((2, nwin, SPAN, GROUP, LANES), BF16),
            vmem((front_cols, width), BF16),
            vmem((front_rows, front_cols), BF16),
            vmem((2, SIDE, SIDE, own, LANES), F32),
            vmem((2, 2, SIDE + 2, own, LANES), jnp.int16),
            vmem((2, 2, SIDE + 2, own, LANES), jnp.int16),
            vmem((2, 3, own, LANES), F32),
            vmem((2, 2, 3, own // 2, LANES), jnp.int16),
            vmem((2, 2, 3, own // 2, LANES), jnp.int16),
            vmem((2, 2, 2, 2, SIDE + 2, 1, LANES), F32),
            vmem((own, width), BF16),
            vmem((nown, own, LANES), F32),
            vmem((SIDE * SIDE, slab, width), F32),
            vmem((SIDE * SIDE - 1, slab, width), F32),
            vmem((slab, width), F32),
            vmem((SPAN, slab, width), F32),
            vmem((SIDE * SIDE, slab, width), F32),
            dma((160,)),
            dma((2, SIDE, SIDE)),
            dma((2, 2, SPAN // 2)),
            dma((2, 2, 2, SIDE + 2)),
            dma((2, 2, 2, 3)),
            dma,
            dma((SIDE * SIDE - 1,)),
            dma((SPAN - 1,)),
            dma((SIDE * SIDE - 1,)),
            dma((5,)),
        ],
        compiler_params=pltpu.CompilerParams(
            collective_id=0, has_side_effects=True, vmem_limit_bytes=60 * 1024 * 1024
        ),
        name="selected_inverse",
    )(
        panel.reshape(block // (SPAN * GROUP), SPAN, GROUP, width),
        row_map.reshape(nchunk, LANES),
        front_inverse,
        diag_inverse[0],
    )
    whole = pl.BlockSpec(memory_space=pltpu.VMEM)
    offdiag, diag = pl.pallas_call(
        finish,
        out_shape=(
            jax.ShapeDtypeStruct((own, width), F32),
            jax.ShapeDtypeStruct((width, width), F32),
        ),
        in_specs=[whole, whole],
        out_specs=(whole, whole),
        name="outputs",
    )(offdiag, diag)
    return offdiag[None], diag[None]


def solution(mesh):
    finer = Mesh(
        mesh.devices.reshape(mesh.shape["sib"], mesh.shape["row"], SIDE, SIDE),
        ("sib", "row", "col_0", "col_1"),
    )
    return jax.shard_map(
        shards,
        mesh=finer,
        in_specs=(P("row", COL), P("sib", COL, None), P("sib", None), P("sib", None, None)),
        out_specs=(P("sib", ROW_COL, None), P("sib", None, None)),
        check_vma=False,
    )
```

```python
import functools

import jax
import jax.numpy as jnp
from jax import lax
from jax.experimental import pallas as pl
from jax.experimental.pallas import tpu as pltpu
from jax.sharding import Mesh
from jax.sharding import PartitionSpec as P

COL = ("col_0", "col_1")
ROW_COL = ("row", "col_0", "col_1")
MESH_ID = pl.DeviceIdType.MESH
LANES = 128
GROUP = 16
LEVELS = 32767.0
TINY = 1e-33
SIDE = 4
SPAN = 8
F32 = jnp.float32
BF16 = jnp.bfloat16


def kernel(
    panel, places_in, front, dinv_in, off_out, diag_out,
    places, dinv, off_v, diag_v, gath, wind, spread, front_v, part, out_1, ring_1, mid, out_2, ring_2, scale, own_s, hits,
    terms, got_d, sum_z, got_z, total,
    send, rg, rz, r1, r2, rs, rd, rzz, rt, loc,
):
    nblk = panel.shape[0]
    nchunk = places.shape[0]
    front_rows, front_cols = front.shape
    ntgt = front_cols // LANES
    nwin = wind.shape[2]
    own = own_s.shape[0]
    z = lax.axis_index("row")
    pos = {"col_0": lax.axis_index("col_0"), "col_1": lax.axis_index("col_1")}
    px, py = pos["col_0"], pos["col_1"]
    col = px * SIDE + py
    order = (("col_0", "col_1"), ("col_1", "col_0"))
    sends = []

    def put(src, dst, sem, **device):
        copy = pltpu.make_async_remote_copy(
            src_ref=src, dst_ref=dst, send_sem=send.at[len(sends)], recv_sem=sem,
            device_id=device, device_id_type=MESH_ID,
        )
        copy.start()
        sends.append(copy)

    def arrive(dst, sem):
        pltpu.make_async_copy(dst, dst, sem).wait()

    def step(axis, delta):
        return {axis: lax.rem(pos[axis] + delta + SIDE, SIDE)}

    def in_plane(off):
        x, y = lax.rem(px + off // SIDE, SIDE), lax.rem(py + off % SIDE, SIDE)
        return x * SIDE + y, {"col_0": x, "col_1": y}

    others = (10, 6, 14, 9, 11, 2, 8, 5, 7, 13, 15, 1, 3, 4, 12)
    planes = (4, 3, 5, 2, 6, 1, 7)

    to_row = col // 2
    to_col = SPAN * lax.rem(col, 2) + z
    from_col = 2 * z + col // SPAN
    from_row = lax.rem(col, SPAN)
    stays = jnp.logical_and(to_row == z, to_col == col)
    goes = jnp.logical_not(stays)
    to_dev = {"row": to_row, "col_0": to_col // SIDE, "col_1": lax.rem(to_col, SIDE)}
    from_dev = {"row": from_row, "col_0": from_col // SIDE, "col_1": lax.rem(from_col, SIDE)}

    load_front = pltpu.make_async_copy(front, front_v, loc.at[0])
    load_front.start()
    load_places = pltpu.make_async_copy(places_in, places, loc.at[5])
    load_places.start()
    load_dinv = pltpu.make_async_copy(dinv_in, dinv, loc.at[6])
    load_dinv.start()

    barrier = pltpu.get_barrier_semaphore()
    for axis in ("col_0", "col_1"):
        for delta in (1, -1, 2):
            pl.semaphore_signal(
                barrier, inc=1, device_id=step(axis, delta), device_id_type=MESH_ID
            )
    for delta in (1, -1):
        pl.semaphore_signal(
            barrier, inc=1, device_id={"row": lax.rem(z + delta + SPAN, SPAN)},
            device_id_type=MESH_ID,
        )
    pl.semaphore_wait(barrier, 2 * (SIDE - 1) + 2)

    def slot(h, d0, d1):
        a0, a1 = order[h]
        c0 = lax.rem(pos[a0] + d0, SIDE)
        c1 = lax.rem(pos[a1] + d1, SIDE)
        k = c0 * SIDE + c1 if h == 0 else c1 * SIDE + c0
        return gath.at[h, pl.ds(k * nblk, nblk)]

    def mine(h):
        return panel.at[:, z, :, pl.ds(h * LANES, LANES)]

    def pass_on(h, d0, d1, which, delta, src=None):
        dst = slot(h, d0, d1)
        d0, d1 = ((d0 - delta) % SIDE, d1) if which == 0 else (d0, (d1 - delta) % SIDE)
        put(dst if src is None else src, dst, rg.at[h, d0, d1], **step(order[h][which], delta))

    def gathered(h, d0, d1):
        arrive(slot(h, d0, d1), rg.at[h, d0, d1])

    for h in range(2):
        for delta in (2, 1, -1):
            pass_on(h, 0, 0, 0, delta, mine(h))
    for h in range(2):
        for delta in (2, 1, -1):
            pass_on(h, 0, 0, 1, delta, mine(h))
    keep = [pltpu.make_async_copy(mine(h), slot(h, 0, 0), loc.at[1 + h]) for h in range(2)]
    for copy in keep:
        copy.start()

    load_places.wait()
    place = places[...]

    def chunk_of(bound):
        return jnp.sum((place < bound).astype(jnp.int32)) // LANES

    col_base = col * front_cols
    chunks = [chunk_of(col_base + t * LANES) for t in range(ntgt)]
    first = jnp.minimum(chunks[0], nchunk - nwin)
    own_base = z * front_rows + col * own
    nown = hits.shape[0]
    own_first = jnp.minimum(chunk_of(own_base), nchunk - nown)
    target = lax.broadcasted_iota(jnp.int32, (own, LANES), 0) + own_base
    mark = jnp.zeros((own, LANES), F32)
    for i in range(nown):
        mark += jnp.where(places[pl.ds(own_first + i, 1), :] == target, 1.0, 0.0)
    hit_rows = jnp.broadcast_to(jnp.max(mark, axis=1, keepdims=True), (own, LANES))
    hits[0] = hit_rows

    for d in (1, 3, 2):
        for h in range(2):
            gathered(h, d, 0)
            for delta in (2, 1, -1):
                pass_on(h, d, 0, 1, delta)
    for copy in keep:
        copy.wait()
    for h in range(2):
        for d in range(SIDE):
            for e in range(1, SIDE):
                gathered(h, d, e)

    for h in range(2):
        for i in range(nwin):
            wind[h, z, i] = gath[h, first + i]

    cuts = ((0, nwin // 2), (nwin // 2, nwin - nwin // 2))

    def share(h, u, d):
        return wind.at[h, lax.rem(z + d + SPAN, SPAN), pl.ds(*cuts[u])]

    last = ((SPAN // 2, SPAN // 2 - 1), (SPAN // 2 - 1, SPAN // 2))
    pieces = [(u, h, d, 1 - 2 * d) for u in range(2) for h in range(2) for d in range(2)]
    for s in range(1, SPAN // 2 + 1):
        for u, h, d, sign in pieces:
            if s <= last[h][d]:
                block = share(h, u, -sign * (s - 1))
                if s > 1:
                    arrive(block, rz.at[h, u, d, s - 2])
                put(block, block, rz.at[h, u, d, s - 1], row=lax.rem(z + sign + SPAN, SPAN))
    for u, h, d, sign in pieces:
        arrive(share(h, u, -sign * last[h][d]), rz.at[h, u, d, last[h][d] - 1])

    rows_at = lax.broadcasted_iota(jnp.int32, (LANES, LANES), 0)
    for t in range(ntgt):
        a = jnp.minimum(chunks[t] - first, nwin - 2)
        want = rows_at + (col_base + t * LANES)
        table = jnp.concatenate(
            [
                jnp.where(places[pl.ds(first + a + i, 1), :] == want, 1.0, 0.0).astype(BF16)
                for i in range(2)
            ],
            axis=1,
        )
        for h in range(2):
            rows = jnp.concatenate(
                [wind[h, :, a + i].reshape(LANES, LANES) for i in range(2)], axis=0
            )
            spread[pl.ds(t * LANES, LANES), pl.ds(h * LANES, LANES)] = jnp.dot(
                table, rows, preferred_element_type=F32
            ).astype(BF16)

    given = spread.at[pl.ds(pl.multiple_of(z * own, GROUP), own)]
    give = pltpu.make_async_remote_copy(
        src_ref=given, dst_ref=own_s, send_sem=loc.at[3], recv_sem=rs,
        device_id=to_dev, device_id_type=MESH_ID,
    )

    @pl.when(goes)
    def _():
        give.start()

    @pl.when(stays)
    def _():
        copy = pltpu.make_async_copy(given, own_s, loc.at[4])
        copy.start()
        copy.wait()

    def post(value, out, dst, at, sem, device):
        top = jnp.maximum(jnp.max(jnp.abs(value), axis=0, keepdims=True), TINY)
        out[...] = jnp.round(value * (LEVELS / top)).astype(jnp.int32).astype(jnp.int16)
        scale[(0, *at)] = top * (1.0 / LEVELS)
        put(scale.at[(0, *at)], scale.at[(1, *at)], sem.at[(1, *at[1:])], **device)
        put(out, dst, sem.at[(0, *at[1:])], **device)

    def fetch(dst, at, sem):
        arrive(scale.at[(1, *at)], sem.at[(1, *at[1:])])
        arrive(dst, sem.at[(0, *at[1:])])
        return dst[...].astype(jnp.int32).astype(F32) * scale[(1, *at)]

    def post_1(value, h, d, at):
        post(value, out_1.at[h, d, at], ring_1.at[h, d, at], (0, h, d, at), r1,
             step(order[h][0], 1 - 2 * d))

    def fetch_1(h, d, at):
        return fetch(ring_1.at[h, d, at], (0, h, d, at), r1)

    def near(h, d, j):
        post_1(part[h, 1 if d == 0 else 3, j], h, d, j)

    def far(h, d, j):
        post_1(part[h, 2, j], h, d, SIDE + j % 2)

    load_front.wait()
    stripe = SIDE * own
    for d in (2, 1, 3, 0):
        at = pl.multiple_of(lax.rem(px + d, SIDE) * stripe, stripe)
        block = jnp.dot(
            front_v[pl.ds(at, stripe), :], spread[...], preferred_element_type=F32
        )
        for y in range(SIDE):
            j = lax.rem(y - py + SIDE, SIDE)
            part[0, d, j] = block[y * own:(y + 1) * own, :LANES]
            part[1, j, d] = block[y * own:(y + 1) * own, LANES:]
        if d == 2:
            for j in range(SIDE):
                far(0, j // 2, j)
        if d == 1:
            near(0, 0, 2)
            near(0, 0, 3)
        if d == 3:
            near(0, 1, 0)
            near(0, 1, 1)
        far(1, d // 2, d)
        near(1, 0 if d >= 2 else 1, d)
    for jj in range(2):
        for h in range(2):
            for d in range(2):
                j = 2 * d + jj
                post_1(part[h, 1 if d == 0 else 3, j] + fetch_1(h, d, SIDE + jj), h, d, j)

    for j in (2, 1, 3, 0):
        for h in range(2):
            both = part[h, 0, j] + fetch_1(h, 0, j) + fetch_1(h, 1, j)
            if j:
                post(both, out_2.at[h, j - 1], ring_2.at[h, j - 1], (1, h, 0, j - 1), r2,
                     step(order[h][1], j))
            else:
                mid[h] = both
    halves = []
    for h in range(2):
        both = mid[h]
        for j in (1, 3, 2):
            both += fetch(ring_2.at[h, j - 1], (1, h, 0, j - 1), r2)
        halves.append(both)
    hit_rows = hits[0]
    for h in range(2):
        off_v[:, pl.ds(h * LANES, LANES)] = jnp.where(hit_rows > 0.5, -halves[h], 0.0)
    save_off = pltpu.make_async_copy(off_v, off_out, loc.at[7])
    save_off.start()
    product = jnp.concatenate(halves, axis=1)

    @pl.when(goes)
    def _():
        give.wait()

    high = product.astype(BF16)
    low = (product - high.astype(F32)).astype(BF16)
    rows = own_s[...]
    dims = (((0,), (0,)), ((), ()))
    here = lax.dot_general(rows, high, dims, preferred_element_type=F32)
    here += lax.dot_general(rows, low, dims, preferred_element_type=F32)
    terms[...] = here.reshape(terms.shape)
    for off in others:
        peer, device = in_plane(off)
        put(terms.at[peer], got_d.at[off - 1], rd.at[off - 1], **device)
    acc = terms[col]
    for off in reversed(others):
        arrive(got_d.at[off - 1], rd.at[off - 1])
        acc += got_d[off - 1]
    sum_z[...] = acc
    for off in planes:
        put(sum_z, got_z.at[off - 1], rzz.at[off - 1], row=lax.rem(z + off, SPAN))
    for off in reversed(planes):
        arrive(got_z.at[off - 1], rzz.at[off - 1])
    acc = jnp.zeros_like(acc)
    got_z[SPAN - 1] = sum_z[...]
    for r in range(SPAN):
        at = lax.rem(z - r + SPAN - 1 + SPAN, SPAN)
        acc += got_z[at]
    total[col] = acc
    for off in others:
        peer, device = in_plane(off)
        put(total.at[col], total.at[col], rt.at[off - 1], **device)
    for off in reversed(others):
        x = lax.rem(px + SIDE - off // SIDE, SIDE)
        y = lax.rem(py + SIDE - off % SIDE, SIDE)
        arrive(total.at[x * SIDE + y], rt.at[off - 1])
    load_dinv.wait()
    diag_v[...] = dinv[...] + total[...].reshape(dinv.shape)
    save_diag = pltpu.make_async_copy(diag_v, diag_out, loc.at[8])
    save_diag.start()
    save_off.wait()
    save_diag.wait()
    for copy in sends:
        copy.wait_send()


def finish(off, diag, off_out, diag_out):
    off_out[...] = off[...]
    diag_out[...] = diag[...]


def shards(front_inverse, panel, row_map, diag_inverse):
    front_rows, front_cols = front_inverse.shape
    _, block, width = panel.shape
    count = row_map.shape[1]
    nchunk = count // LANES
    nwin = front_cols // LANES + 1
    own = front_rows // (SIDE * SIDE)
    nown = (own + 2 * LANES - 2) // LANES
    slab = width // (SIDE * SIDE)
    vmem = pltpu.VMEM
    dma = pltpu.SemaphoreType.DMA
    offdiag, diag = pl.pallas_call(
        kernel,
        out_shape=(
            jax.ShapeDtypeStruct((own, width), F32),
            jax.ShapeDtypeStruct((width, width), F32),
        ),
        in_specs=[
            pl.BlockSpec(memory_space=pl.ANY),
            pl.BlockSpec(memory_space=pl.ANY),
            pl.BlockSpec(memory_space=pl.ANY),
            pl.BlockSpec(memory_space=pl.ANY),
        ],
        out_specs=(
            pl.BlockSpec(memory_space=pl.ANY),
            pl.BlockSpec(memory_space=pl.ANY),
        ),
        scratch_shapes=[
            vmem((nchunk, LANES), jnp.int32),
            vmem((width, width), F32),
            vmem((own, width), F32),
            vmem((width, width), F32),
            vmem((2, nchunk, GROUP, LANES), BF16),
            vmem((2, SPAN, nwin, GROUP, LANES), BF16),
            vmem((front_cols, width), BF16),
            vmem((front_rows, front_cols), BF16),
            vmem((2, SIDE, SIDE, own, LANES), F32),
            vmem((2, 2, SIDE + 2, own, LANES), jnp.int16),
            vmem((2, 2, SIDE + 2, own, LANES), jnp.int16),
            vmem((2, own, LANES), F32),
            vmem((2, SIDE - 1, own, LANES), jnp.int16),
            vmem((2, SIDE - 1, own, LANES), jnp.int16),
            vmem((2, 2, 2, 2, SIDE + 2, 1, LANES), F32),
            vmem((own, width), BF16),
            vmem((nown, own, LANES), F32),
            vmem((SIDE * SIDE, slab, width), F32),
            vmem((SIDE * SIDE - 1, slab, width), F32),
            vmem((slab, width), F32),
            vmem((SPAN, slab, width), F32),
            vmem((SIDE * SIDE, slab, width), F32),
            dma((160,)),
            dma((2, SIDE, SIDE)),
            dma((2, 2, 2, SPAN // 2)),
            dma((2, 2, 2, SIDE + 2)),
            dma((2, 2, 1, SIDE - 1)),
            dma,
            dma((SIDE * SIDE - 1,)),
            dma((SPAN - 1,)),
            dma((SIDE * SIDE - 1,)),
            dma((9,)),
        ],
        compiler_params=pltpu.CompilerParams(
            collective_id=0, has_side_effects=True, vmem_limit_bytes=60 * 1024 * 1024
        ),
        name="selected_inverse",
    )(
        panel.reshape(block // (SPAN * GROUP), SPAN, GROUP, width),
        row_map.reshape(nchunk, LANES),
        front_inverse,
        diag_inverse[0],
    )
    whole = pl.BlockSpec(memory_space=pltpu.VMEM)
    offdiag, diag = pl.pallas_call(
        finish,
        out_shape=(
            jax.ShapeDtypeStruct((own, width), F32),
            jax.ShapeDtypeStruct((width, width), F32),
        ),
        in_specs=[whole, whole],
        out_specs=(whole, whole),
        name="outputs",
    )(offdiag, diag)
    return offdiag[None], diag[None]


def solution(mesh):
    finer = Mesh(
        mesh.devices.reshape(mesh.shape["sib"], mesh.shape["row"], SIDE, SIDE),
        ("sib", "row", "col_0", "col_1"),
    )
    return jax.shard_map(
        shards,
        mesh=finer,
        in_specs=(P("row", COL), P("sib", COL, None), P("sib", None), P("sib", None, None)),
        out_specs=(P("sib", ROW_COL, None), P("sib", None, None)),
        check_vma=False,
    )
```

```python
import functools

import jax
import jax.numpy as jnp
from jax import lax
from jax.experimental import pallas as pl
from jax.experimental.pallas import tpu as pltpu
from jax.sharding import Mesh
from jax.sharding import PartitionSpec as P

COL = ("col_0", "col_1")
ROW_COL = ("row", "col_0", "col_1")
MESH_ID = pl.DeviceIdType.MESH
LANES = 128
GROUP = 16
LEVELS = 32767.0
TINY = 1e-33
SIDE = 4
SPAN = 8
F32 = jnp.float32
BF16 = jnp.bfloat16


def kernel(
    panel, places_in, front, dinv_in, off_out, diag_out,
    places, dinv, gath, wind, spread, front_v, part, out_1, ring_1, mid, out_2, ring_2, scale, own_s, hits,
    terms, got_d, sum_z, got_z, total,
    send, rg, rz, r1, r2, rs, rd, rzz, rt, loc,
):
    nblk = panel.shape[0]
    nchunk = places.shape[0]
    front_rows, front_cols = front.shape
    ntgt = front_cols // LANES
    nwin = wind.shape[2]
    own = own_s.shape[0]
    z = lax.axis_index("row")
    pos = {"col_0": lax.axis_index("col_0"), "col_1": lax.axis_index("col_1")}
    px, py = pos["col_0"], pos["col_1"]
    col = px * SIDE + py
    order = (("col_0", "col_1"), ("col_1", "col_0"))
    def put(src, dst, out, sem, **device):
        pltpu.make_async_remote_copy(
            src_ref=src, dst_ref=dst, send_sem=send.at[out], recv_sem=sem,
            device_id=device, device_id_type=MESH_ID,
        ).start()

    def arrive(dst, sem):
        pltpu.make_async_copy(dst, dst, sem).wait()

    def sent(same_bytes, out):
        pltpu.make_async_copy(same_bytes, same_bytes, send.at[out]).wait()

    def step(axis, delta):
        return {axis: lax.rem(pos[axis] + delta + SIDE, SIDE)}

    def in_plane(off):
        x, y = lax.rem(px + off // SIDE, SIDE), lax.rem(py + off % SIDE, SIDE)
        return x * SIDE + y, {"col_0": x, "col_1": y}

    others = (10, 6, 14, 9, 11, 2, 8, 5, 7, 13, 15, 1, 3, 4, 12)
    planes = (4, 3, 5, 2, 6, 1, 7)

    to_row = col // 2
    to_col = SPAN * lax.rem(col, 2) + z
    from_col = 2 * z + col // SPAN
    from_row = lax.rem(col, SPAN)
    stays = jnp.logical_and(to_row == z, to_col == col)
    goes = jnp.logical_not(stays)
    to_dev = {"row": to_row, "col_0": to_col // SIDE, "col_1": lax.rem(to_col, SIDE)}
    from_dev = {"row": from_row, "col_0": from_col // SIDE, "col_1": lax.rem(from_col, SIDE)}

    load_front = pltpu.make_async_copy(front, front_v, loc.at[0])
    load_front.start()
    load_places = pltpu.make_async_copy(places_in, places, loc.at[5])
    load_places.start()
    load_dinv = pltpu.make_async_copy(dinv_in, dinv, loc.at[6])
    load_dinv.start()

    barrier = pltpu.get_barrier_semaphore()
    for axis in ("col_0", "col_1"):
        for delta in (1, -1, 2):
            pl.semaphore_signal(
                barrier, inc=1, device_id=step(axis, delta), device_id_type=MESH_ID
            )
    for delta in (2, -2, 1, -1):
        pl.semaphore_signal(
            barrier, inc=1, device_id={"row": lax.rem(z + delta + SPAN, SPAN)},
            device_id_type=MESH_ID,
        )
    pl.semaphore_wait(barrier, 2 * (SIDE - 1) + 4)

    def slot(h, d0, d1):
        a0, a1 = order[h]
        c0 = lax.rem(pos[a0] + d0, SIDE)
        c1 = lax.rem(pos[a1] + d1, SIDE)
        k = c0 * SIDE + c1 if h == 0 else c1 * SIDE + c0
        return gath.at[h, pl.ds(k * nblk, nblk)]

    def mine(h):
        return panel.at[:, z, :, pl.ds(h * LANES, LANES)]

    def pass_on(h, d0, d1, which, delta, src=None):
        dst = slot(h, d0, d1)
        sem = rg.at[h, 0 if which else (d0 - delta) % SIDE]
        put(dst if src is None else src, dst, h, sem, **step(order[h][which], delta))

    def gathered(h, d0):
        arrive(slot(h, d0, 0), rg.at[h, d0])

    for h in range(2):
        for delta in (2, 1, -1):
            pass_on(h, 0, 0, 0, delta, mine(h))
    for h in range(2):
        for delta in (2, 1, -1):
            pass_on(h, 0, 0, 1, delta, mine(h))
    keep = [pltpu.make_async_copy(mine(h), slot(h, 0, 0), loc.at[1 + h]) for h in range(2)]
    for copy in keep:
        copy.start()

    load_places.wait()
    place = places[...]

    def chunk_of(bound):
        return jnp.sum((place < bound).astype(jnp.int32)) // LANES

    col_base = col * front_cols
    chunks = [chunk_of(col_base + t * LANES) for t in range(ntgt)]
    first = jnp.minimum(chunks[0], nchunk - nwin)
    own_base = z * front_rows + col * own
    nown = hits.shape[0]
    own_first = jnp.minimum(chunk_of(own_base), nchunk - nown)
    target = lax.broadcasted_iota(jnp.int32, (own, LANES), 0) + own_base
    mark = jnp.zeros((own, LANES), F32)
    for i in range(nown):
        mark += jnp.where(places[pl.ds(own_first + i, 1), :] == target, 1.0, 0.0)
    hit_rows = jnp.broadcast_to(jnp.max(mark, axis=1, keepdims=True), (own, LANES))
    hits[0] = hit_rows

    for d in (1, 3, 2):
        for h in range(2):
            gathered(h, d)
            for delta in (2, 1, -1):
                pass_on(h, d, 0, 1, delta)
    for copy in keep:
        copy.wait()
    for h in range(2):
        arrive(gath.at[h, pl.ds(0, SIDE * (SIDE - 1) * nblk)], rg.at[h, 0])

    for h in range(2):
        for i in range(nwin):
            wind[h, z, i] = gath[h, first + i]

    cuts = ((0, nwin // 2), (nwin // 2, nwin - nwin // 2))

    def share(h, u, d):
        return wind.at[h, lax.rem(z + d + SPAN, SPAN), pl.ds(*cuts[u])]

    pieces = [(u, h, d, 1 - 2 * d) for u in range(2) for h in range(2) for d in range(2)]

    def pass_z(u, h, d, sign, origin, hops):
        block = share(h, u, -sign * origin)
        put(block, block, 2 + 2 * u + h, rz.at[h, u, d, origin + hops - 1],
            row=lax.rem(z + sign * hops + SPAN, SPAN))

    def came_z(u, h, d, sign, origin):
        arrive(share(h, u, -sign * origin), rz.at[h, u, d, origin - 1])

    for u, h, d, sign in pieces:
        if h != d:
            pass_z(u, h, d, sign, 0, 1)
    for u, h, d, sign in pieces:
        if h == d:
            pass_z(u, h, d, sign, 0, 2)
    for u, h, d, sign in pieces:
        if h == d:
            pass_z(u, h, d, sign, 0, 1)
    for u, h, d, sign in pieces:
        if h != d:
            came_z(u, h, d, sign, 1)
            pass_z(u, h, d, sign, 1, 1)
    for u, h, d, sign in pieces:
        if h == d:
            came_z(u, h, d, sign, 2)
            pass_z(u, h, d, sign, 2, 1)
    for u, h, d, sign in pieces:
        if h != d:
            came_z(u, h, d, sign, 2)
            pass_z(u, h, d, sign, 2, 1)
    for u, h, d, sign in pieces:
        if h == d:
            came_z(u, h, d, sign, 3)
            pass_z(u, h, d, sign, 3, 1)
    for u, h, d, sign in pieces:
        if h == d:
            came_z(u, h, d, sign, 1)
            came_z(u, h, d, sign, 4)
        else:
            came_z(u, h, d, sign, 3)

    rows_at = lax.broadcasted_iota(jnp.int32, (LANES, LANES), 0)
    for t in range(ntgt):
        a = jnp.minimum(chunks[t] - first, nwin - 2)
        want = rows_at + (col_base + t * LANES)
        table = jnp.concatenate(
            [
                jnp.where(places[pl.ds(first + a + i, 1), :] == want, 1.0, 0.0).astype(BF16)
                for i in range(2)
            ],
            axis=1,
        )
        for h in range(2):
            rows = jnp.concatenate(
                [wind[h, :, a + i].reshape(LANES, LANES) for i in range(2)], axis=0
            )
            spread[pl.ds(t * LANES, LANES), pl.ds(h * LANES, LANES)] = jnp.dot(
                table, rows, preferred_element_type=F32
            ).astype(BF16)

    given = spread.at[pl.ds(pl.multiple_of(z * own, GROUP), own)]
    give = pltpu.make_async_remote_copy(
        src_ref=given, dst_ref=own_s, send_sem=loc.at[3], recv_sem=rs,
        device_id=to_dev, device_id_type=MESH_ID,
    )

    @pl.when(goes)
    def _():
        give.start()

    @pl.when(stays)
    def _():
        copy = pltpu.make_async_copy(given, own_s, loc.at[4])
        copy.start()
        copy.wait()

    def post(value, out, dst, at, sem, device, sems):
        top = jnp.maximum(jnp.max(jnp.abs(value), axis=0, keepdims=True), TINY)
        out[...] = jnp.round(value * (LEVELS / top)).astype(jnp.int32).astype(jnp.int16)
        scale[(0, *at)] = top * (1.0 / LEVELS)
        put(scale.at[(0, *at)], scale.at[(1, *at)], sems[1], sem[1], **device)
        put(out, dst, sems[0], sem[0], **device)

    def value_of(dst, at):
        return dst[...].astype(jnp.int32).astype(F32) * scale[(1, *at)]

    def post_1(value, h, d, at):
        post(value, out_1.at[h, d, at], ring_1.at[h, d, at], (0, h, d, at),
             (r1.at[0, h, d, at], r1.at[1, h, d, at]), step(order[h][0], 1 - 2 * d),
             (6 + h, 8 + h))

    def fetch_1(h, d, at):
        arrive(scale.at[1, 0, h, d, at], r1.at[1, h, d, at])
        arrive(ring_1.at[h, d, at], r1.at[0, h, d, at])
        return value_of(ring_1.at[h, d, at], (0, h, d, at))

    def near(h, d, j):
        post_1(part[h, 1 if d == 0 else 3, j], h, d, j)

    def far(h, d, j):
        post_1(part[h, 2, j], h, d, SIDE + j % 2)

    load_front.wait()

    def rows_of(dx, dy):
        at = (lax.rem(px + dx, SIDE) * SIDE + lax.rem(py + dy, SIDE)) * own
        return front_v[pl.ds(pl.multiple_of(at, GROUP), own), :]

    def multiply(*blocks):
        rows = jnp.concatenate([rows_of(*block) for block in blocks], axis=0)
        whole = jnp.dot(rows, spread[...], preferred_element_type=F32)
        for n, (dx, dy) in enumerate(blocks):
            part[0, dx, dy] = whole[n * own:(n + 1) * own, :LANES]
            part[1, dy, dx] = whole[n * own:(n + 1) * own, LANES:]

    multiply((2, 0), (2, 2), (2, 1), (2, 3))
    for j in (0, 2, 1, 3):
        far(0, j // 2, j)
    far(1, 1, 2)
    near(1, 0, 2)
    multiply((0, 2), (1, 2), (3, 2))
    for j in (0, 1, 3):
        far(1, j // 2, j)
    near(0, 0, 2)
    multiply((1, 3), (3, 1), (3, 0), (0, 3))
    for h in range(2):
        near(h, 0, 3)
        near(h, 1, 0)
        near(h, 1, 1)
    multiply((1, 0), (0, 1), (3, 3), (1, 1), (0, 0))
    for jj in range(2):
        for h in range(2):
            for d in range(2):
                j = 2 * d + jj
                post_1(part[h, 1 if d == 0 else 3, j] + fetch_1(h, d, SIDE + jj), h, d, j)

    for j in (2, 1, 3, 0):
        for h in range(2):
            both = part[h, 0, j] + fetch_1(h, 0, j) + fetch_1(h, 1, j)
            if j:
                post(both, out_2.at[h, j - 1], ring_2.at[h, j - 1], (1, h, 0, j - 1),
                     (r2.at[0, h], r2.at[1, h]), step(order[h][1], j), (10 + h, 12 + h))
            else:
                mid[h] = both
    halves = []
    for h in range(2):
        arrive(scale.at[1, 1, h, 0, pl.ds(0, SIDE - 1)], r2.at[1, h])
        arrive(ring_2.at[h], r2.at[0, h])
        both = mid[h]
        for j in (1, 3, 2):
            both += value_of(ring_2.at[h, j - 1], (1, h, 0, j - 1))
        halves.append(both)
    hit_rows = hits[0]
    for h in range(2):
        off_out[:, pl.ds(h * LANES, LANES)] = jnp.where(hit_rows > 0.5, -halves[h], 0.0)
    product = jnp.concatenate(halves, axis=1)

    @pl.when(goes)
    def _():
        give.wait()

    high = product.astype(BF16)
    low = (product - high.astype(F32)).astype(BF16)
    rows = own_s[...]
    dims = (((0,), (0,)), ((), ()))
    here = lax.dot_general(rows, high, dims, preferred_element_type=F32)
    here += lax.dot_general(rows, low, dims, preferred_element_type=F32)
    terms[...] = here.reshape(terms.shape)
    for off in others:
        peer, device = in_plane(off)
        put(terms.at[peer], got_d.at[off - 1], 14, rd, **device)
    acc = terms[col]
    arrive(got_d, rd)
    for off in others:
        acc += got_d[off - 1]
    sum_z[...] = acc
    for off in planes:
        put(sum_z, got_z.at[off - 1], 15, rzz, row=lax.rem(z + off, SPAN))
    arrive(got_z.at[pl.ds(0, SPAN - 1)], rzz)
    acc = jnp.zeros_like(acc)
    got_z[SPAN - 1] = sum_z[...]
    for r in range(SPAN):
        at = lax.rem(z - r + SPAN - 1 + SPAN, SPAN)
        acc += got_z[at]
    total[col] = acc
    for off in others:
        peer, device = in_plane(off)
        put(total.at[col], total.at[col], 16, rt, **device)
    arrive(total.at[pl.ds(0, SIDE * SIDE - 1)], rt)
    load_dinv.wait()
    diag_out[...] = dinv[...] + total[...].reshape(dinv.shape)
    for h in range(2):
        sent(gath.at[h, pl.ds(0, (SIDE * SIDE - 1) * nblk)], h)
        for u in range(2):
            sent(gath.at[h, pl.ds(0, (SPAN - 1) * cuts[u][1])], 2 + 2 * u + h)
        sent(out_1.at[h], 6 + h)
        sent(scale.at[0, 0, h], 8 + h)
        sent(out_2.at[h], 10 + h)
        sent(scale.at[0, 1, h, 0, pl.ds(0, SIDE - 1)], 12 + h)
    sent(got_d, 14)
    sent(got_z.at[pl.ds(0, SPAN - 1)], 15)
    sent(total.at[pl.ds(0, SIDE * SIDE - 1)], 16)


def finish(off, diag, off_out, diag_out, sems):
    copies = [
        pltpu.make_async_copy(off, off_out, sems.at[0]),
        pltpu.make_async_copy(diag, diag_out, sems.at[1]),
    ]
    for copy in copies:
        copy.start()
    for copy in copies:
        copy.wait()


def shards(front_inverse, panel, row_map, diag_inverse):
    front_rows, front_cols = front_inverse.shape
    _, block, width = panel.shape
    count = row_map.shape[1]
    nchunk = count // LANES
    nwin = front_cols // LANES + 1
    own = front_rows // (SIDE * SIDE)
    nown = (own + 2 * LANES - 2) // LANES
    slab = width // (SIDE * SIDE)
    vmem = pltpu.VMEM
    dma = pltpu.SemaphoreType.DMA
    offdiag, diag = pl.pallas_call(
        kernel,
        out_shape=(
            jax.ShapeDtypeStruct((own, width), F32),
            jax.ShapeDtypeStruct((width, width), F32),
        ),
        in_specs=[pl.BlockSpec(memory_space=pltpu.HBM)] * 4,
        out_specs=(pl.BlockSpec(memory_space=pltpu.VMEM),) * 2,
        scratch_shapes=[
            vmem((nchunk, LANES), jnp.int32),
            vmem((width, width), F32),
            vmem((2, nchunk, GROUP, LANES), BF16),
            vmem((2, SPAN, nwin, GROUP, LANES), BF16),
            vmem((front_cols, width), BF16),
            vmem((front_rows, front_cols), BF16),
            vmem((2, SIDE, SIDE, own, LANES), F32),
            vmem((2, 2, SIDE + 2, own, LANES), jnp.int16),
            vmem((2, 2, SIDE + 2, own, LANES), jnp.int16),
            vmem((2, own, LANES), F32),
            vmem((2, SIDE - 1, own, LANES), jnp.int16),
            vmem((2, SIDE - 1, own, LANES), jnp.int16),
            vmem((2, 2, 2, 2, SIDE + 2, 1, LANES), F32),
            vmem((own, width), BF16),
            vmem((nown, own, LANES), F32),
            vmem((SIDE * SIDE, slab, width), F32),
            vmem((SIDE * SIDE - 1, slab, width), F32),
            vmem((slab, width), F32),
            vmem((SPAN, slab, width), F32),
            vmem((SIDE * SIDE, slab, width), F32),
            dma((17,)),
            dma((2, SIDE)),
            dma((2, 2, 2, SPAN // 2)),
            dma((2, 2, 2, SIDE + 2)),
            dma((2, 2)),
            dma,
            dma,
            dma,
            dma,
            dma((7,)),
        ],
        compiler_params=pltpu.CompilerParams(
            collective_id=0, has_side_effects=True, vmem_limit_bytes=32 * 1024 * 1024
        ),
        name="selected_inverse",
    )(
        *(
            pltpu.with_memory_space_constraint(x, pltpu.HBM)
            for x in (
                panel.reshape(block // (SPAN * GROUP), SPAN, GROUP, width),
                row_map.reshape(nchunk, LANES),
                front_inverse,
                diag_inverse[0],
            )
        )
    )
    whole = pl.BlockSpec(memory_space=pl.ANY)
    offdiag, diag = pl.pallas_call(
        finish,
        out_shape=(
            jax.ShapeDtypeStruct((own, width), F32),
            jax.ShapeDtypeStruct((width, width), F32),
        ),
        in_specs=[whole, whole],
        out_specs=(whole, whole),
        scratch_shapes=[dma((2,))],
        name="outputs",
    )(*(pltpu.with_memory_space_constraint(x, pltpu.VMEM) for x in (offdiag, diag)))
    return offdiag[None], diag[None]


def solution(mesh):
    finer = Mesh(
        mesh.devices.reshape(mesh.shape["sib"], mesh.shape["row"], SIDE, SIDE),
        ("sib", "row", "col_0", "col_1"),
    )
    return jax.shard_map(
        shards,
        mesh=finer,
        in_specs=(P("row", COL), P("sib", COL, None), P("sib", None), P("sib", None, None)),
        out_specs=(P("sib", ROW_COL, None), P("sib", None, None)),
        check_vma=False,
    )
```

```python
import functools

import jax
import jax.numpy as jnp
from jax import lax
from jax.experimental import pallas as pl
from jax.experimental.pallas import tpu as pltpu
from jax.sharding import Mesh
from jax.sharding import PartitionSpec as P

COL = ("col_0", "col_1")
ROW_COL = ("row", "col_0", "col_1")
MESH_ID = pl.DeviceIdType.MESH
LANES = 128
GROUP = 16
LEVELS = 32767.0
TINY = 1e-33
SIDE = 4
SPAN = 8
F32 = jnp.float32
BF16 = jnp.bfloat16


def kernel(
    panel, places_in, front, dinv_in, off_out, diag_out,
    places, dinv, gath, wind, spread, front_v, part, out_1, ring_1, mid, out_2, ring_2, scale, own_s, hits,
    terms, got_d, got_z, total, dscale,
    send, rg, rz, r1, r2, rs, rd, rzz, rt, loc,
):
    nblk = panel.shape[0]
    nchunk = places.shape[0]
    front_rows, front_cols = front.shape
    ntgt = front_cols // LANES
    nwin = wind.shape[2]
    own = own_s.shape[0]
    z = lax.axis_index("row")
    pos = {"col_0": lax.axis_index("col_0"), "col_1": lax.axis_index("col_1")}
    px, py = pos["col_0"], pos["col_1"]
    col = px * SIDE + py
    order = (("col_0", "col_1"), ("col_1", "col_0"))
    def put(src, dst, out, sem, **device):
        pltpu.make_async_remote_copy(
            src_ref=src, dst_ref=dst, send_sem=send.at[out], recv_sem=sem,
            device_id=device, device_id_type=MESH_ID,
        ).start()

    def arrive(dst, sem):
        pltpu.make_async_copy(dst, dst, sem).wait()

    def sent(same_bytes, out):
        pltpu.make_async_copy(same_bytes, same_bytes, send.at[out]).wait()

    def step(axis, delta):
        return {axis: lax.rem(pos[axis] + delta + SIDE, SIDE)}

    def in_plane(off):
        x, y = lax.rem(px + off // SIDE, SIDE), lax.rem(py + off % SIDE, SIDE)
        return x * SIDE + y, {"col_0": x, "col_1": y}

    others = (10, 6, 14, 9, 11, 2, 8, 5, 7, 13, 15, 1, 3, 4, 12)
    planes = (4, 3, 5, 2, 6, 1, 7)

    to_row = col // 2
    to_col = SPAN * lax.rem(col, 2) + z
    from_col = 2 * z + col // SPAN
    from_row = lax.rem(col, SPAN)
    stays = jnp.logical_and(to_row == z, to_col == col)
    goes = jnp.logical_not(stays)
    to_dev = {"row": to_row, "col_0": to_col // SIDE, "col_1": lax.rem(to_col, SIDE)}
    from_dev = {"row": from_row, "col_0": from_col // SIDE, "col_1": lax.rem(from_col, SIDE)}

    load_front = pltpu.make_async_copy(front, front_v, loc.at[0])
    load_front.start()
    load_places = pltpu.make_async_copy(places_in, places, loc.at[5])
    load_places.start()
    load_dinv = pltpu.make_async_copy(dinv_in, dinv, loc.at[6])
    load_dinv.start()

    barrier = pltpu.get_barrier_semaphore()
    for axis in ("col_0", "col_1"):
        for delta in (1, -1, 2):
            pl.semaphore_signal(
                barrier, inc=1, device_id=step(axis, delta), device_id_type=MESH_ID
            )
    for delta in (2, -2, 1, -1):
        pl.semaphore_signal(
            barrier, inc=1, device_id={"row": lax.rem(z + delta + SPAN, SPAN)},
            device_id_type=MESH_ID,
        )
    pl.semaphore_wait(barrier, 2 * (SIDE - 1) + 4)

    def slot(h, d0, d1):
        a0, a1 = order[h]
        c0 = lax.rem(pos[a0] + d0, SIDE)
        c1 = lax.rem(pos[a1] + d1, SIDE)
        k = c0 * SIDE + c1 if h == 0 else c1 * SIDE + c0
        return gath.at[h, pl.ds(k * nblk, nblk)]

    def mine(h):
        return panel.at[:, z, :, pl.ds(h * LANES, LANES)]

    def pass_on(h, d0, d1, which, delta, src=None):
        dst = slot(h, d0, d1)
        sem = rg.at[h, 0 if which else (d0 - delta) % SIDE]
        put(dst if src is None else src, dst, h, sem, **step(order[h][which], delta))

    def gathered(h, d0):
        arrive(slot(h, d0, 0), rg.at[h, d0])

    for h in range(2):
        for delta in (2, 1, -1):
            pass_on(h, 0, 0, 0, delta, mine(h))
    for h in range(2):
        for delta in (2, 1, -1):
            pass_on(h, 0, 0, 1, delta, mine(h))
    keep = [pltpu.make_async_copy(mine(h), slot(h, 0, 0), loc.at[1 + h]) for h in range(2)]
    for copy in keep:
        copy.start()

    load_places.wait()
    place = places[...]

    def chunk_of(bound):
        return jnp.sum((place < bound).astype(jnp.int32)) // LANES

    col_base = col * front_cols
    chunks = [chunk_of(col_base + t * LANES) for t in range(ntgt)]
    first = jnp.minimum(chunks[0], nchunk - nwin)
    own_base = z * front_rows + col * own
    nown = hits.shape[0]
    own_first = jnp.minimum(chunk_of(own_base), nchunk - nown)
    target = lax.broadcasted_iota(jnp.int32, (own, LANES), 0) + own_base
    mark = jnp.zeros((own, LANES), F32)
    for i in range(nown):
        mark += jnp.where(places[pl.ds(own_first + i, 1), :] == target, 1.0, 0.0)
    hit_rows = jnp.broadcast_to(jnp.max(mark, axis=1, keepdims=True), (own, LANES))
    hits[0] = hit_rows

    for d in (1, 3, 2):
        for h in range(2):
            gathered(h, d)
            for delta in (2, 1, -1):
                pass_on(h, d, 0, 1, delta)
    for copy in keep:
        copy.wait()
    for h in range(2):
        arrive(gath.at[h, pl.ds(0, SIDE * (SIDE - 1) * nblk)], rg.at[h, 0])

    for h in range(2):
        for i in range(nwin):
            wind[h, z, i] = gath[h, first + i]

    cuts = ((0, nwin // 2), (nwin // 2, nwin - nwin // 2))

    def share(h, u, d):
        return wind.at[h, lax.rem(z + d + SPAN, SPAN), pl.ds(*cuts[u])]

    pieces = [(u, h, d, 1 - 2 * d) for u in range(2) for h in range(2) for d in range(2)]

    def pass_z(u, h, d, sign, origin, hops):
        block = share(h, u, -sign * origin)
        put(block, block, 2 + 2 * u + h, rz.at[h, u, d, origin + hops - 1],
            row=lax.rem(z + sign * hops + SPAN, SPAN))

    def came_z(u, h, d, sign, origin):
        arrive(share(h, u, -sign * origin), rz.at[h, u, d, origin - 1])

    for u, h, d, sign in pieces:
        if h != d:
            pass_z(u, h, d, sign, 0, 1)
    for u, h, d, sign in pieces:
        if h == d:
            pass_z(u, h, d, sign, 0, 2)
    for u, h, d, sign in pieces:
        if h == d:
            pass_z(u, h, d, sign, 0, 1)
    for u, h, d, sign in pieces:
        if h != d:
            came_z(u, h, d, sign, 1)
            pass_z(u, h, d, sign, 1, 1)
    for u, h, d, sign in pieces:
        if h == d:
            came_z(u, h, d, sign, 2)
            pass_z(u, h, d, sign, 2, 1)
    for u, h, d, sign in pieces:
        if h != d:
            came_z(u, h, d, sign, 2)
            pass_z(u, h, d, sign, 2, 1)
    for u, h, d, sign in pieces:
        if h == d:
            came_z(u, h, d, sign, 3)
            pass_z(u, h, d, sign, 3, 1)
    for u, h, d, sign in pieces:
        if h == d:
            came_z(u, h, d, sign, 1)
            came_z(u, h, d, sign, 4)
        else:
            came_z(u, h, d, sign, 3)

    rows_at = lax.broadcasted_iota(jnp.int32, (LANES, LANES), 0)
    for t in range(ntgt):
        a = jnp.minimum(chunks[t] - first, nwin - 2)
        want = rows_at + (col_base + t * LANES)
        table = jnp.concatenate(
            [
                jnp.where(places[pl.ds(first + a + i, 1), :] == want, 1.0, 0.0).astype(BF16)
                for i in range(2)
            ],
            axis=1,
        )
        for h in range(2):
            rows = jnp.concatenate(
                [wind[h, :, a + i].reshape(LANES, LANES) for i in range(2)], axis=0
            )
            spread[pl.ds(t * LANES, LANES), pl.ds(h * LANES, LANES)] = jnp.dot(
                table, rows, preferred_element_type=F32
            ).astype(BF16)

    given = spread.at[pl.ds(pl.multiple_of(z * own, GROUP), own)]
    give = pltpu.make_async_remote_copy(
        src_ref=given, dst_ref=own_s, send_sem=loc.at[3], recv_sem=rs,
        device_id=to_dev, device_id_type=MESH_ID,
    )

    @pl.when(goes)
    def _():
        give.start()

    @pl.when(stays)
    def _():
        copy = pltpu.make_async_copy(given, own_s, loc.at[4])
        copy.start()
        copy.wait()

    def post(value, out, dst, at, sem, device, sems):
        top = jnp.maximum(jnp.max(jnp.abs(value), axis=0, keepdims=True), TINY)
        out[...] = jnp.round(value * (LEVELS / top)).astype(jnp.int32).astype(jnp.int16)
        scale[(0, *at)] = top * (1.0 / LEVELS)
        put(scale.at[(0, *at)], scale.at[(1, *at)], sems[1], sem[1], **device)
        put(out, dst, sems[0], sem[0], **device)

    def value_of(dst, at):
        return dst[...].astype(jnp.int32).astype(F32) * scale[(1, *at)]

    def post_1(value, h, d, at):
        post(value, out_1.at[h, d, at], ring_1.at[h, d, at], (0, h, d, at),
             (r1.at[0, h, d, at], r1.at[1, h, d, at]), step(order[h][0], 1 - 2 * d),
             (6 + h, 8 + h))

    def fetch_1(h, d, at):
        arrive(scale.at[1, 0, h, d, at], r1.at[1, h, d, at])
        arrive(ring_1.at[h, d, at], r1.at[0, h, d, at])
        return value_of(ring_1.at[h, d, at], (0, h, d, at))

    def near(h, d, j):
        post_1(part[h, 1 if d == 0 else 3, j], h, d, j)

    def far(h, d, j):
        post_1(part[h, 2, j], h, d, SIDE + j % 2)

    load_front.wait()

    def rows_of(dx, dy):
        at = (lax.rem(px + dx, SIDE) * SIDE + lax.rem(py + dy, SIDE)) * own
        return front_v[pl.ds(pl.multiple_of(at, GROUP), own), :]

    def multiply(*blocks):
        rows = jnp.concatenate([rows_of(*block) for block in blocks], axis=0)
        whole = jnp.dot(rows, spread[...], preferred_element_type=F32)
        for n, (dx, dy) in enumerate(blocks):
            part[0, dx, dy] = whole[n * own:(n + 1) * own, :LANES]
            part[1, dy, dx] = whole[n * own:(n + 1) * own, LANES:]

    multiply((2, 2))
    for h in range(2):
        far(h, 1, 2)
    multiply((2, 1), (1, 2), (2, 3), (3, 2))
    for j in (1, 3):
        for h in range(2):
            far(h, j // 2, j)
    for h in range(2):
        near(h, 0, 2)
    multiply((2, 0), (0, 2), (1, 3), (3, 1))
    for h in range(2):
        far(h, 0, 0)
    for h in range(2):
        near(h, 1, 1)
        near(h, 0, 3)
    multiply((3, 0), (0, 3))
    for h in range(2):
        near(h, 1, 0)
    multiply((3, 3), (1, 1), (1, 0), (0, 1), (0, 0))
    for j in (2, 1, 3, 0):
        for h in range(2):
            d = j // 2
            post_1(part[h, 1 if d == 0 else 3, j] + fetch_1(h, d, SIDE + j % 2), h, d, j)

    for j in (2, 1, 3, 0):
        for h in range(2):
            both = part[h, 0, j] + fetch_1(h, 0, j) + fetch_1(h, 1, j)
            if j:
                post(both, out_2.at[h, j - 1], ring_2.at[h, j - 1], (1, h, 0, j - 1),
                     (r2.at[0, h], r2.at[1, h]), step(order[h][1], j), (10 + h, 12 + h))
            else:
                mid[h] = both
    halves = []
    for h in range(2):
        arrive(scale.at[1, 1, h, 0, pl.ds(0, SIDE - 1)], r2.at[1, h])
        arrive(ring_2.at[h], r2.at[0, h])
        both = mid[h]
        for j in (1, 3, 2):
            both += value_of(ring_2.at[h, j - 1], (1, h, 0, j - 1))
        halves.append(both)
    hit_rows = hits[0]
    for h in range(2):
        off_out[:, pl.ds(h * LANES, LANES)] = jnp.where(hit_rows > 0.5, -halves[h], 0.0)
    product = jnp.concatenate(halves, axis=1)

    @pl.when(goes)
    def _():
        give.wait()

    high = product.astype(BF16)
    low = (product - high.astype(F32)).astype(BF16)
    rows = own_s[...]
    dims = (((0,), (0,)), ((), ()))
    here = lax.dot_general(rows, high, dims, preferred_element_type=F32)
    here += lax.dot_general(rows, low, dims, preferred_element_type=F32)

    def code(value):
        top = jnp.maximum(jnp.max(jnp.abs(value), axis=-2, keepdims=True), TINY)
        levels = jnp.round(value * (LEVELS / top)).astype(jnp.int32).astype(jnp.int16)
        return levels, top * (1.0 / LEVELS)

    def plain(levels, unit):
        return levels.astype(jnp.int32).astype(F32) * unit

    here = here.reshape(terms.shape)
    terms[...], dscale[0] = code(here)
    for off in others:
        peer, device = in_plane(off)
        put(dscale.at[0, peer], dscale.at[1, off - 1], 17, rd.at[1], **device)
        put(terms.at[peer], got_d.at[off - 1], 14, rd.at[0], **device)
    acc = plain(terms[col], dscale[0, col])
    arrive(dscale.at[1, pl.ds(0, SIDE * SIDE - 1)], rd.at[1])
    arrive(got_d, rd.at[0])
    for off in others:
        acc += plain(got_d[off - 1], dscale[1, off - 1])
    got_z[SPAN - 1], dscale[2, SPAN - 1] = code(acc)
    for off in planes:
        peer = lax.rem(z + off, SPAN)
        put(dscale.at[2, SPAN - 1], dscale.at[2, off - 1], 18, rzz.at[1], row=peer)
        put(got_z.at[SPAN - 1], got_z.at[off - 1], 15, rzz.at[0], row=peer)
    arrive(dscale.at[2, pl.ds(0, SPAN - 1)], rzz.at[1])
    arrive(got_z.at[pl.ds(0, SPAN - 1)], rzz.at[0])
    acc = jnp.zeros_like(acc)
    for r in range(SPAN):
        at = lax.rem(z - r + SPAN - 1 + SPAN, SPAN)
        acc += plain(got_z[at], dscale[2, at])
    total[col], dscale[3, col] = code(acc)
    for off in others:
        peer, device = in_plane(off)
        put(dscale.at[3, col], dscale.at[3, col], 19, rt.at[1], **device)
        put(total.at[col], total.at[col], 16, rt.at[0], **device)
    arrive(dscale.at[3, pl.ds(0, SIDE * SIDE - 1)], rt.at[1])
    arrive(total.at[pl.ds(0, SIDE * SIDE - 1)], rt.at[0])
    load_dinv.wait()
    diag_out[...] = dinv[...] + plain(total[...], dscale[3]).reshape(dinv.shape)
    for h in range(2):
        sent(gath.at[h, pl.ds(0, (SIDE * SIDE - 1) * nblk)], h)
        for u in range(2):
            sent(gath.at[h, pl.ds(0, (SPAN - 1) * cuts[u][1])], 2 + 2 * u + h)
        sent(out_1.at[h], 6 + h)
        sent(scale.at[0, 0, h], 8 + h)
        sent(out_2.at[h], 10 + h)
        sent(scale.at[0, 1, h, 0, pl.ds(0, SIDE - 1)], 12 + h)
    sent(got_d, 14)
    sent(got_z.at[pl.ds(0, SPAN - 1)], 15)
    for at in (17, 19):
        sent(dscale.at[1, pl.ds(0, SIDE * SIDE - 1)], at)
    sent(dscale.at[2, pl.ds(0, SPAN - 1)], 18)
    sent(total.at[pl.ds(0, SIDE * SIDE - 1)], 16)


def finish(off, diag, off_out, diag_out, sems):
    copies = [
        pltpu.make_async_copy(off, off_out, sems.at[0]),
        pltpu.make_async_copy(diag, diag_out, sems.at[1]),
    ]
    for copy in copies:
        copy.start()
    for copy in copies:
        copy.wait()


def shards(front_inverse, panel, row_map, diag_inverse):
    front_rows, front_cols = front_inverse.shape
    _, block, width = panel.shape
    count = row_map.shape[1]
    nchunk = count // LANES
    nwin = front_cols // LANES + 1
    own = front_rows // (SIDE * SIDE)
    nown = (own + 2 * LANES - 2) // LANES
    slab = width // (SIDE * SIDE)
    vmem = pltpu.VMEM
    dma = pltpu.SemaphoreType.DMA
    offdiag, diag = pl.pallas_call(
        kernel,
        out_shape=(
            jax.ShapeDtypeStruct((own, width), F32),
            jax.ShapeDtypeStruct((width, width), F32),
        ),
        in_specs=[pl.BlockSpec(memory_space=pltpu.HBM)] * 4,
        out_specs=(pl.BlockSpec(memory_space=pltpu.VMEM),) * 2,
        scratch_shapes=[
            vmem((nchunk, LANES), jnp.int32),
            vmem((width, width), F32),
            vmem((2, nchunk, GROUP, LANES), BF16),
            vmem((2, SPAN, nwin, GROUP, LANES), BF16),
            vmem((front_cols, width), BF16),
            vmem((front_rows, front_cols), BF16),
            vmem((2, SIDE, SIDE, own, LANES), F32),
            vmem((2, 2, SIDE + 2, own, LANES), jnp.int16),
            vmem((2, 2, SIDE + 2, own, LANES), jnp.int16),
            vmem((2, own, LANES), F32),
            vmem((2, SIDE - 1, own, LANES), jnp.int16),
            vmem((2, SIDE - 1, own, LANES), jnp.int16),
            vmem((2, 2, 2, 2, SIDE + 2, 1, LANES), F32),
            vmem((own, width), BF16),
            vmem((nown, own, LANES), F32),
            vmem((SIDE * SIDE, slab, width), jnp.int16),
            vmem((SIDE * SIDE - 1, slab, width), jnp.int16),
            vmem((SPAN, slab, width), jnp.int16),
            vmem((SIDE * SIDE, slab, width), jnp.int16),
            vmem((4, SIDE * SIDE, 1, width), F32),
            dma((20,)),
            dma((2, SIDE)),
            dma((2, 2, 2, SPAN // 2)),
            dma((2, 2, 2, SIDE + 2)),
            dma((2, 2)),
            dma,
            dma((2,)),
            dma((2,)),
            dma((2,)),
            dma((7,)),
        ],
        compiler_params=pltpu.CompilerParams(
            collective_id=0, has_side_effects=True, vmem_limit_bytes=32 * 1024 * 1024
        ),
        name="selected_inverse",
    )(
        *(
            pltpu.with_memory_space_constraint(x, pltpu.HBM)
            for x in (
                panel.reshape(block // (SPAN * GROUP), SPAN, GROUP, width),
                row_map.reshape(nchunk, LANES),
                front_inverse,
                diag_inverse[0],
            )
        )
    )
    whole = pl.BlockSpec(memory_space=pl.ANY)
    offdiag, diag = pl.pallas_call(
        finish,
        out_shape=(
            jax.ShapeDtypeStruct((own, width), F32),
            jax.ShapeDtypeStruct((width, width), F32),
        ),
        in_specs=[whole, whole],
        out_specs=(whole, whole),
        scratch_shapes=[dma((2,))],
        name="outputs",
    )(*(pltpu.with_memory_space_constraint(x, pltpu.VMEM) for x in (offdiag, diag)))
    return offdiag[None], diag[None]


def solution(mesh):
    finer = Mesh(
        mesh.devices.reshape(mesh.shape["sib"], mesh.shape["row"], SIDE, SIDE),
        ("sib", "row", "col_0", "col_1"),
    )
    return jax.shard_map(
        shards,
        mesh=finer,
        in_specs=(P("row", COL), P("sib", COL, None), P("sib", None), P("sib", None, None)),
        out_specs=(P("sib", ROW_COL, None), P("sib", None, None)),
        check_vma=False,
    )
```

```python
import functools

import jax
import jax.numpy as jnp
from jax import lax
from jax.experimental import pallas as pl
from jax.experimental.pallas import tpu as pltpu
from jax.sharding import Mesh
from jax.sharding import PartitionSpec as P

COL = ("col_0", "col_1")
ROW_COL = ("row", "col_0", "col_1")
MESH_ID = pl.DeviceIdType.MESH
LANES = 128
GROUP = 16
LEVELS = 32767.0
TINY = 1e-33
SIDE = 4
SPAN = 8
F32 = jnp.float32
BF16 = jnp.bfloat16


def kernel(
    panel, places_in, front, dinv_in, off_out, diag_out,
    places, dinv, gath, wind, spread, front_v, part, out_1, ring_1, mid, out_2, ring_2, scale, own_s, hits,
    terms, got_d, got_z, total, dscale,
    send, rg, rz, r1, r2, rs, rd, rzz, rt, loc,
):
    nblk = panel.shape[0]
    nchunk = places.shape[0]
    front_rows, front_cols = front.shape
    ntgt = front_cols // LANES
    nwin = wind.shape[2]
    own = own_s.shape[0]
    z = lax.axis_index("row")
    pos = {"col_0": lax.axis_index("col_0"), "col_1": lax.axis_index("col_1")}
    px, py = pos["col_0"], pos["col_1"]
    col = px * SIDE + py
    order = (("col_0", "col_1"), ("col_1", "col_0"))
    def put(src, dst, out, sem, **device):
        pltpu.make_async_remote_copy(
            src_ref=src, dst_ref=dst, send_sem=send.at[out], recv_sem=sem,
            device_id=device, device_id_type=MESH_ID,
        ).start()

    def arrive(dst, sem):
        pltpu.make_async_copy(dst, dst, sem).wait()

    def sent(same_bytes, out):
        pltpu.make_async_copy(same_bytes, same_bytes, send.at[out]).wait()

    def step(axis, delta):
        return {axis: lax.rem(pos[axis] + delta + SIDE, SIDE)}

    def in_plane(off):
        x, y = lax.rem(px + off // SIDE, SIDE), lax.rem(py + off % SIDE, SIDE)
        return x * SIDE + y, {"col_0": x, "col_1": y}

    others = (10, 6, 14, 9, 11, 2, 8, 5, 7, 13, 15, 1, 3, 4, 12)
    planes = (4, 3, 5, 2, 6, 1, 7)

    to_row = col // 2
    to_col = SPAN * lax.rem(col, 2) + z
    from_col = 2 * z + col // SPAN
    from_row = lax.rem(col, SPAN)
    stays = jnp.logical_and(to_row == z, to_col == col)
    goes = jnp.logical_not(stays)
    to_dev = {"row": to_row, "col_0": to_col // SIDE, "col_1": lax.rem(to_col, SIDE)}
    from_dev = {"row": from_row, "col_0": from_col // SIDE, "col_1": lax.rem(from_col, SIDE)}

    load_front = pltpu.make_async_copy(front, front_v, loc.at[0])
    load_front.start()
    load_places = pltpu.make_async_copy(places_in, places, loc.at[5])
    load_places.start()
    load_dinv = pltpu.make_async_copy(dinv_in, dinv, loc.at[6])
    load_dinv.start()

    barrier = pltpu.get_barrier_semaphore()
    for axis in ("col_0", "col_1"):
        for delta in (1, -1, 2):
            pl.semaphore_signal(
                barrier, inc=1, device_id=step(axis, delta), device_id_type=MESH_ID
            )
    for delta in (2, -2, 1, -1):
        pl.semaphore_signal(
            barrier, inc=1, device_id={"row": lax.rem(z + delta + SPAN, SPAN)},
            device_id_type=MESH_ID,
        )
    pl.semaphore_wait(barrier, 2 * (SIDE - 1) + 4)

    def slot(h, d0, d1):
        a0, a1 = order[h]
        c0 = lax.rem(pos[a0] + d0, SIDE)
        c1 = lax.rem(pos[a1] + d1, SIDE)
        k = c0 * SIDE + c1 if h == 0 else c1 * SIDE + c0
        return gath.at[h, pl.ds(k * nblk, nblk)]

    def mine(h):
        return panel.at[:, z, :, pl.ds(h * LANES, LANES)]

    def pass_on(h, d0, d1, which, delta, src=None):
        dst = slot(h, d0, d1)
        sem = rg.at[h, 0 if which else (d0 - delta) % SIDE]
        put(dst if src is None else src, dst, 0, sem, **step(order[h][which], delta))

    def gathered(h, d0):
        arrive(slot(h, d0, 0), rg.at[h, d0])

    for h in range(2):
        for delta in (2, 1, -1):
            pass_on(h, 0, 0, 0, delta, mine(h))
    for h in range(2):
        for delta in (2, 1, -1):
            pass_on(h, 0, 0, 1, delta, mine(h))
    keep = [pltpu.make_async_copy(mine(h), slot(h, 0, 0), loc.at[1 + h]) for h in range(2)]
    for copy in keep:
        copy.start()

    load_places.wait()
    place = places[...]

    def chunk_of(bound):
        return jnp.sum((place < bound).astype(jnp.int32)) // LANES

    col_base = col * front_cols
    chunks = [chunk_of(col_base + t * LANES) for t in range(ntgt)]
    first = jnp.minimum(chunks[0], nchunk - nwin)
    own_base = z * front_rows + col * own
    nown = hits.shape[0]
    own_first = jnp.minimum(chunk_of(own_base), nchunk - nown)
    target = lax.broadcasted_iota(jnp.int32, (own, LANES), 0) + own_base
    mark = jnp.zeros((own, LANES), F32)
    for i in range(nown):
        mark += jnp.where(places[pl.ds(own_first + i, 1), :] == target, 1.0, 0.0)
    hit_rows = jnp.broadcast_to(jnp.max(mark, axis=1, keepdims=True), (own, LANES))
    hits[0] = hit_rows

    for d in (1, 3, 2):
        for h in range(2):
            gathered(h, d)
            for delta in (2, 1, -1):
                pass_on(h, d, 0, 1, delta)
    for copy in keep:
        copy.wait()
    for h in range(2):
        arrive(gath.at[h, pl.ds(0, SIDE * (SIDE - 1) * nblk)], rg.at[h, 0])

    for h in range(2):
        for i in range(nwin):
            wind[h, z, i] = gath[h, first + i]

    cuts = ((0, nwin // 2), (nwin // 2, nwin - nwin // 2))

    def share(h, u, d):
        return wind.at[h, lax.rem(z + d + SPAN, SPAN), pl.ds(*cuts[u])]

    pieces = [(u, h, d, 1 - 2 * d) for u in range(2) for h in range(2) for d in range(2)]

    def pass_z(u, h, d, sign, origin, hops):
        block = share(h, u, -sign * origin)
        put(block, block, 1 + u, rz.at[h, u, d, origin + hops - 1],
            row=lax.rem(z + sign * hops + SPAN, SPAN))

    def came_z(u, h, d, sign, origin):
        arrive(share(h, u, -sign * origin), rz.at[h, u, d, origin - 1])

    for u, h, d, sign in pieces:
        if h != d:
            pass_z(u, h, d, sign, 0, 1)
    for u, h, d, sign in pieces:
        if h == d:
            pass_z(u, h, d, sign, 0, 2)
    for u, h, d, sign in pieces:
        if h == d:
            pass_z(u, h, d, sign, 0, 1)
    for u, h, d, sign in pieces:
        if h != d:
            came_z(u, h, d, sign, 1)
            pass_z(u, h, d, sign, 1, 1)
    for u, h, d, sign in pieces:
        if h == d:
            came_z(u, h, d, sign, 2)
            pass_z(u, h, d, sign, 2, 2)
    for u, h, d, sign in pieces:
        if h == d:
            pass_z(u, h, d, sign, 2, 1)
    for u, h, d, sign in pieces:
        if h != d:
            came_z(u, h, d, sign, 2)
            pass_z(u, h, d, sign, 2, 1)
    for u, h, d, sign in pieces:
        if h == d:
            came_z(u, h, d, sign, 1)
            came_z(u, h, d, sign, 3)
            came_z(u, h, d, sign, 4)
        else:
            came_z(u, h, d, sign, 3)

    rows_at = lax.broadcasted_iota(jnp.int32, (LANES, LANES), 0)
    for t in range(ntgt):
        a = jnp.minimum(chunks[t] - first, nwin - 2)
        want = rows_at + (col_base + t * LANES)
        table = jnp.concatenate(
            [
                jnp.where(places[pl.ds(first + a + i, 1), :] == want, 1.0, 0.0).astype(BF16)
                for i in range(2)
            ],
            axis=1,
        )
        for h in range(2):
            rows = jnp.concatenate(
                [wind[h, :, a + i].reshape(LANES, LANES) for i in range(2)], axis=0
            )
            spread[pl.ds(t * LANES, LANES), pl.ds(h * LANES, LANES)] = jnp.dot(
                table, rows, preferred_element_type=F32
            ).astype(BF16)

    given = spread.at[pl.ds(pl.multiple_of(z * own, GROUP), own)]
    give = pltpu.make_async_remote_copy(
        src_ref=given, dst_ref=own_s, send_sem=loc.at[3], recv_sem=rs,
        device_id=to_dev, device_id_type=MESH_ID,
    )

    @pl.when(goes)
    def _():
        give.start()

    @pl.when(stays)
    def _():
        copy = pltpu.make_async_copy(given, own_s, loc.at[4])
        copy.start()
        copy.wait()

    def post(value, out, dst, at, sem, device, sems):
        top = jnp.maximum(jnp.max(jnp.abs(value), axis=0, keepdims=True), TINY)
        out[...] = jnp.round(value * (LEVELS / top)).astype(jnp.int32).astype(jnp.int16)
        scale[(0, *at)] = top * (1.0 / LEVELS)
        put(scale.at[(0, *at)], scale.at[(1, *at)], sems[1], sem[1], **device)
        put(out, dst, sems[0], sem[0], **device)

    def value_of(dst, at):
        return dst[...].astype(jnp.int32).astype(F32) * scale[(1, *at)]

    def post_1(value, h, d, at, sem):
        post(value, out_1.at[h, d, at], ring_1.at[h, d, at], (0, h, d, at),
             (r1.at[0, h, sem], r1.at[1, h, sem]), step(order[h][0], 1 - 2 * d), (3, 4))

    def fetch_far(h, j):
        d, at = j // 2, SIDE + j % 2
        arrive(scale.at[1, 0, h, d, at], r1.at[1, h, SIDE + j])
        arrive(ring_1.at[h, d, at], r1.at[0, h, SIDE + j])
        return value_of(ring_1.at[h, d, at], (0, h, d, at))

    def fetch_near(h, j):
        arrive(scale.at[1, 0, h, :, j], r1.at[1, h, j])
        arrive(ring_1.at[h, :, j], r1.at[0, h, j])
        return [value_of(ring_1.at[h, d, j], (0, h, d, j)) for d in range(2)]

    def near(h, d, j):
        post_1(part[h, 1 if d == 0 else 3, j], h, d, j, j)

    def far(h, d, j):
        post_1(part[h, 2, j], h, d, SIDE + j % 2, SIDE + j)

    load_front.wait()

    def rows_of(dx, dy):
        at = (lax.rem(px + dx, SIDE) * SIDE + lax.rem(py + dy, SIDE)) * own
        return front_v[pl.ds(pl.multiple_of(at, GROUP), own), :]

    def multiply(*blocks):
        rows = jnp.concatenate([rows_of(*block) for block in blocks], axis=0)
        whole = jnp.dot(rows, spread[...], preferred_element_type=F32)
        for n, (dx, dy) in enumerate(blocks):
            part[0, dx, dy] = whole[n * own:(n + 1) * own, :LANES]
            part[1, dy, dx] = whole[n * own:(n + 1) * own, LANES:]

    multiply((2, 2))
    for h in range(2):
        far(h, 1, 2)
    multiply((2, 1), (1, 2), (2, 3), (3, 2))
    for j in (1, 3):
        for h in range(2):
            far(h, j // 2, j)
    for h in range(2):
        near(h, 0, 2)
    multiply((2, 0), (0, 2), (1, 3), (3, 1))
    for h in range(2):
        far(h, 0, 0)
    for h in range(2):
        near(h, 1, 1)
        near(h, 0, 3)
    multiply((3, 0), (0, 3))
    for h in range(2):
        near(h, 1, 0)
    multiply((3, 3), (1, 1), (1, 0), (0, 1), (0, 0))
    for j in (2, 1, 3, 0):
        for h in range(2):
            d = j // 2
            post_1(part[h, 1 if d == 0 else 3, j] + fetch_far(h, j), h, d, j, j)

    for j in (2, 1, 3, 0):
        for h in range(2):
            ahead, behind = fetch_near(h, j)
            both = part[h, 0, j] + ahead + behind
            if j:
                post(both, out_2.at[h, j - 1], ring_2.at[h, j - 1], (1, h, 0, j - 1),
                     (r2.at[0, h], r2.at[1, h]), step(order[h][1], j), (5, 6))
            else:
                mid[h] = both
    halves = []
    for h in range(2):
        arrive(scale.at[1, 1, h, 0, pl.ds(0, SIDE - 1)], r2.at[1, h])
        arrive(ring_2.at[h], r2.at[0, h])
        both = mid[h]
        for j in (1, 3, 2):
            both += value_of(ring_2.at[h, j - 1], (1, h, 0, j - 1))
        halves.append(both)
    hit_rows = hits[0]
    for h in range(2):
        off_out[:, pl.ds(h * LANES, LANES)] = jnp.where(hit_rows > 0.5, -halves[h], 0.0)
    product = jnp.concatenate(halves, axis=1)

    @pl.when(goes)
    def _():
        give.wait()

    high = product.astype(BF16)
    low = (product - high.astype(F32)).astype(BF16)
    rows = own_s[...]
    dims = (((0,), (0,)), ((), ()))
    here = lax.dot_general(rows, high, dims, preferred_element_type=F32)
    here += lax.dot_general(rows, low, dims, preferred_element_type=F32)

    def code(value):
        top = jnp.maximum(jnp.max(jnp.abs(value), axis=-2, keepdims=True), TINY)
        levels = jnp.round(value * (LEVELS / top)).astype(jnp.int32).astype(jnp.int16)
        return levels, top * (1.0 / LEVELS)

    def plain(levels, unit):
        return levels.astype(jnp.int32).astype(F32) * unit

    here = here.reshape(terms.shape)
    terms[...], dscale[0] = code(here)
    for off in others:
        peer, device = in_plane(off)
        put(dscale.at[0, peer], dscale.at[1, off - 1], 8, rd.at[1], **device)
        put(terms.at[peer], got_d.at[off - 1], 7, rd.at[0], **device)
    acc = plain(terms[col], dscale[0, col])
    arrive(dscale.at[1, pl.ds(0, SIDE * SIDE - 1)], rd.at[1])
    arrive(got_d, rd.at[0])
    for off in others:
        acc += plain(got_d[off - 1], dscale[1, off - 1])
    got_z[SPAN - 1], dscale[2, SPAN - 1] = code(acc)
    for off in planes:
        peer = lax.rem(z + off, SPAN)
        put(dscale.at[2, SPAN - 1], dscale.at[2, off - 1], 10, rzz.at[1], row=peer)
        put(got_z.at[SPAN - 1], got_z.at[off - 1], 9, rzz.at[0], row=peer)
    arrive(dscale.at[2, pl.ds(0, SPAN - 1)], rzz.at[1])
    arrive(got_z.at[pl.ds(0, SPAN - 1)], rzz.at[0])
    acc = jnp.zeros_like(acc)
    for r in range(SPAN):
        at = lax.rem(z - r + SPAN - 1 + SPAN, SPAN)
        acc += plain(got_z[at], dscale[2, at])
    total[col], dscale[3, col] = code(acc)
    for off in others:
        peer, device = in_plane(off)
        put(dscale.at[3, col], dscale.at[3, col], 12, rt.at[1], **device)
        put(total.at[col], total.at[col], 11, rt.at[0], **device)
    arrive(dscale.at[3, pl.ds(0, SIDE * SIDE - 1)], rt.at[1])
    arrive(total.at[pl.ds(0, SIDE * SIDE - 1)], rt.at[0])
    load_dinv.wait()
    diag_out[...] = dinv[...] + plain(total[...], dscale[3]).reshape(dinv.shape)
    sent(gath.at[:, pl.ds(0, (SIDE * SIDE - 1) * nblk)], 0)
    for u in range(2):
        sent(gath.at[:, pl.ds(0, (SPAN - 1) * cuts[u][1])], 1 + u)
    sent(out_1, 3)
    sent(scale.at[0, 0], 4)
    sent(out_2, 5)
    sent(scale.at[0, 1, :, 0, pl.ds(0, SIDE - 1)], 6)
    sent(got_d, 7)
    sent(dscale.at[1, pl.ds(0, SIDE * SIDE - 1)], 8)
    sent(got_z.at[pl.ds(0, SPAN - 1)], 9)
    sent(dscale.at[2, pl.ds(0, SPAN - 1)], 10)
    sent(dscale.at[3, pl.ds(0, SIDE * SIDE - 1)], 12)
    sent(total.at[pl.ds(0, SIDE * SIDE - 1)], 11)


def finish(off, diag, off_out, diag_out, sems):
    copies = [
        pltpu.make_async_copy(off, off_out, sems.at[0]),
        pltpu.make_async_copy(diag, diag_out, sems.at[1]),
    ]
    for copy in copies:
        copy.start()
    for copy in copies:
        copy.wait()


def shards(front_inverse, panel, row_map, diag_inverse):
    front_rows, front_cols = front_inverse.shape
    _, block, width = panel.shape
    count = row_map.shape[1]
    nchunk = count // LANES
    nwin = front_cols // LANES + 1
    own = front_rows // (SIDE * SIDE)
    nown = (own + 2 * LANES - 2) // LANES
    slab = width // (SIDE * SIDE)
    vmem = pltpu.VMEM
    dma = pltpu.SemaphoreType.DMA
    offdiag, diag = pl.pallas_call(
        kernel,
        out_shape=(
            jax.ShapeDtypeStruct((own, width), F32),
            jax.ShapeDtypeStruct((width, width), F32),
        ),
        in_specs=[pl.BlockSpec(memory_space=pltpu.HBM)] * 4,
        out_specs=(pl.BlockSpec(memory_space=pltpu.VMEM),) * 2,
        scratch_shapes=[
            vmem((nchunk, LANES), jnp.int32),
            vmem((width, width), F32),
            vmem((2, nchunk, GROUP, LANES), BF16),
            vmem((2, SPAN, nwin, GROUP, LANES), BF16),
            vmem((front_cols, width), BF16),
            vmem((front_rows, front_cols), BF16),
            vmem((2, SIDE, SIDE, own, LANES), F32),
            vmem((2, 2, SIDE + 2, own, LANES), jnp.int16),
            vmem((2, 2, SIDE + 2, own, LANES), jnp.int16),
            vmem((2, own, LANES), F32),
            vmem((2, SIDE - 1, own, LANES), jnp.int16),
            vmem((2, SIDE - 1, own, LANES), jnp.int16),
            vmem((2, 2, 2, 2, SIDE + 2, 1, LANES), F32),
            vmem((own, width), BF16),
            vmem((nown, own, LANES), F32),
            vmem((SIDE * SIDE, slab, width), jnp.int16),
            vmem((SIDE * SIDE - 1, slab, width), jnp.int16),
            vmem((SPAN, slab, width), jnp.int16),
            vmem((SIDE * SIDE, slab, width), jnp.int16),
            vmem((4, SIDE * SIDE, 1, width), F32),
            dma((13,)),
            dma((2, SIDE)),
            dma((2, 2, 2, SPAN // 2)),
            dma((2, 2, 2 * SIDE)),
            dma((2, 2)),
            dma,
            dma((2,)),
            dma((2,)),
            dma((2,)),
            dma((7,)),
        ],
        compiler_params=pltpu.CompilerParams(
            collective_id=0, has_side_effects=True, vmem_limit_bytes=32 * 1024 * 1024
        ),
        name="selected_inverse",
    )(
        *(
            pltpu.with_memory_space_constraint(x, pltpu.HBM)
            for x in (
                panel.reshape(block // (SPAN * GROUP), SPAN, GROUP, width),
                row_map.reshape(nchunk, LANES),
                front_inverse,
                diag_inverse[0],
            )
        )
    )
    whole = pl.BlockSpec(memory_space=pl.ANY)
    offdiag, diag = pl.pallas_call(
        finish,
        out_shape=(
            jax.ShapeDtypeStruct((own, width), F32),
            jax.ShapeDtypeStruct((width, width), F32),
        ),
        in_specs=[whole, whole],
        out_specs=(whole, whole),
        scratch_shapes=[dma((2,))],
        name="outputs",
    )(*(pltpu.with_memory_space_constraint(x, pltpu.VMEM) for x in (offdiag, diag)))
    return offdiag[None], diag[None]


def solution(mesh):
    finer = Mesh(
        mesh.devices.reshape(mesh.shape["sib"], mesh.shape["row"], SIDE, SIDE),
        ("sib", "row", "col_0", "col_1"),
    )
    return jax.shard_map(
        shards,
        mesh=finer,
        in_specs=(P("row", COL), P("sib", COL, None), P("sib", None), P("sib", None, None)),
        out_specs=(P("sib", ROW_COL, None), P("sib", None, None)),
        check_vma=False,
    )
```

```python
import functools

import jax
import jax.numpy as jnp
from jax import lax
from jax.experimental import pallas as pl
from jax.experimental.pallas import tpu as pltpu
from jax.sharding import Mesh
from jax.sharding import PartitionSpec as P

COL = ("col_0", "col_1")
ROW_COL = ("row", "col_0", "col_1")
MESH_ID = pl.DeviceIdType.MESH
LANES = 128
GROUP = 16
LEVELS = 32767.0
TINY = 1e-33
SIDE = 4
SPAN = 8
F32 = jnp.float32
BF16 = jnp.bfloat16


def kernel(
    panel, places_in, front, dinv_in, off_out, diag_out,
    places, dinv, gath, wind, spread, front_v, part, out_1, ring_1, mid, out_2, ring_2, scale, own_s, hits,
    terms, got_d, got_z, total, dscale,
    send, rg, rz, r1, r2, rs, rd, rzz, rt, loc,
):
    nblk = panel.shape[0]
    nchunk = places.shape[0]
    front_rows, front_cols = front.shape
    ntgt = front_cols // LANES
    nwin = wind.shape[2]
    own = own_s.shape[0]
    z = lax.axis_index("row")
    pos = {"col_0": lax.axis_index("col_0"), "col_1": lax.axis_index("col_1")}
    px, py = pos["col_0"], pos["col_1"]
    col = px * SIDE + py
    order = (("col_0", "col_1"), ("col_1", "col_0"))
    def put(src, dst, out, sem, **device):
        pltpu.make_async_remote_copy(
            src_ref=src, dst_ref=dst, send_sem=send.at[out], recv_sem=sem,
            device_id=device, device_id_type=MESH_ID,
        ).start()

    def arrive(dst, sem):
        pltpu.make_async_copy(dst, dst, sem).wait()

    def sent(same_bytes, out):
        pltpu.make_async_copy(same_bytes, same_bytes, send.at[out]).wait()

    def step(axis, delta):
        return {axis: lax.rem(pos[axis] + delta + SIDE, SIDE)}

    def in_plane(off):
        x, y = lax.rem(px + off // SIDE, SIDE), lax.rem(py + off % SIDE, SIDE)
        return x * SIDE + y, {"col_0": x, "col_1": y}

    others = (10, 6, 14, 9, 11, 2, 8, 5, 7, 13, 15, 1, 3, 4, 12)
    planes = (4, 3, 5, 2, 6, 1, 7)

    to_row = col // 2
    to_col = SPAN * lax.rem(col, 2) + z
    from_col = 2 * z + col // SPAN
    from_row = lax.rem(col, SPAN)
    stays = jnp.logical_and(to_row == z, to_col == col)
    goes = jnp.logical_not(stays)
    to_dev = {"row": to_row, "col_0": to_col // SIDE, "col_1": lax.rem(to_col, SIDE)}
    from_dev = {"row": from_row, "col_0": from_col // SIDE, "col_1": lax.rem(from_col, SIDE)}

    barrier = pltpu.get_barrier_semaphore()
    for axis in ("col_0", "col_1"):
        for delta in (2, 1, -1):
            pl.semaphore_signal(
                barrier, inc=1, device_id=step(axis, delta), device_id_type=MESH_ID
            )
    for delta in (2, -2, 1, -1):
        pl.semaphore_signal(
            barrier, inc=1, device_id={"row": lax.rem(z + delta + SPAN, SPAN)},
            device_id_type=MESH_ID,
        )
    load_front = pltpu.make_async_copy(front, front_v, loc.at[0])
    load_front.start()
    load_places = pltpu.make_async_copy(places_in, places, loc.at[5])
    load_places.start()
    load_dinv = pltpu.make_async_copy(dinv_in, dinv, loc.at[6])
    load_dinv.start()
    pl.semaphore_wait(barrier, 2 * (SIDE - 1) + 4)

    def slot(h, d0, d1):
        a0, a1 = order[h]
        c0 = lax.rem(pos[a0] + d0, SIDE)
        c1 = lax.rem(pos[a1] + d1, SIDE)
        k = c0 * SIDE + c1 if h == 0 else c1 * SIDE + c0
        return gath.at[h, pl.ds(k * nblk, nblk)]

    def mine(h):
        return panel.at[:, z, :, pl.ds(h * LANES, LANES)]

    def pass_on(h, d0, d1, which, delta, src=None):
        dst = slot(h, d0, d1)
        sem = rg.at[h, 0 if which else (d0 - delta) % SIDE]
        put(dst if src is None else src, dst, 0, sem, **step(order[h][which], delta))

    def gathered(h, d0):
        arrive(slot(h, d0, 0), rg.at[h, d0])

    for h in range(2):
        for delta in (2, 1, -1):
            pass_on(h, 0, 0, 0, delta, mine(h))
    for h in range(2):
        for delta in (2, 1, -1):
            pass_on(h, 0, 0, 1, delta, mine(h))
    keep = [pltpu.make_async_copy(mine(h), slot(h, 0, 0), loc.at[1 + h]) for h in range(2)]
    for copy in keep:
        copy.start()

    load_places.wait()
    place = places[...]

    def chunk_of(bound):
        return jnp.sum((place < bound).astype(jnp.int32)) // LANES

    col_base = col * front_cols
    chunks = [chunk_of(col_base + t * LANES) for t in range(ntgt)]
    first = jnp.minimum(chunks[0], nchunk - nwin)
    own_base = z * front_rows + col * own
    nown = hits.shape[0]
    own_first = jnp.minimum(chunk_of(own_base), nchunk - nown)
    target = lax.broadcasted_iota(jnp.int32, (own, LANES), 0) + own_base
    mark = jnp.zeros((own, LANES), F32)
    for i in range(nown):
        mark += jnp.where(places[pl.ds(own_first + i, 1), :] == target, 1.0, 0.0)
    hit_rows = jnp.broadcast_to(jnp.max(mark, axis=1, keepdims=True), (own, LANES))
    hits[0] = hit_rows

    for d in (1, 3, 2):
        for h in range(2):
            gathered(h, d)
            for delta in (2, 1, -1):
                pass_on(h, d, 0, 1, delta)
    for copy in keep:
        copy.wait()
    for h in range(2):
        arrive(gath.at[h, pl.ds(0, SIDE * (SIDE - 1) * nblk)], rg.at[h, 0])

    for h in range(2):
        for i in range(nwin):
            wind[h, z, i] = gath[h, first + i]

    cuts = ((0, nwin // 2), (nwin // 2, nwin - nwin // 2))

    def share(h, u, d):
        return wind.at[h, lax.rem(z + d + SPAN, SPAN), pl.ds(*cuts[u])]

    pieces = [(u, h, d, 1 - 2 * d) for u in range(2) for h in range(2) for d in range(2)]

    def pass_z(u, h, d, sign, origin, hops):
        block = share(h, u, -sign * origin)
        put(block, block, 1 + u, rz.at[h, u, d, origin + hops - 1],
            row=lax.rem(z + sign * hops + SPAN, SPAN))

    def came_z(u, h, d, sign, origin):
        arrive(share(h, u, -sign * origin), rz.at[h, u, d, origin - 1])

    for u, h, d, sign in pieces:
        if h != d:
            pass_z(u, h, d, sign, 0, 1)
    for u, h, d, sign in pieces:
        if h == d:
            pass_z(u, h, d, sign, 0, 2)
    for u, h, d, sign in pieces:
        if h != d:
            came_z(u, h, d, sign, 1)
            pass_z(u, h, d, sign, 1, 1)
    for u, h, d, sign in pieces:
        if h == d:
            pass_z(u, h, d, sign, 0, 1)
    for u, h, d, sign in pieces:
        if h == d:
            came_z(u, h, d, sign, 2)
            pass_z(u, h, d, sign, 2, 2)
    for u, h, d, sign in pieces:
        if h == d:
            pass_z(u, h, d, sign, 2, 1)
    for u, h, d, sign in pieces:
        if h != d:
            came_z(u, h, d, sign, 2)
            pass_z(u, h, d, sign, 2, 1)
    for u, h, d, sign in pieces:
        if h == d:
            came_z(u, h, d, sign, 1)
            came_z(u, h, d, sign, 3)
            came_z(u, h, d, sign, 4)
        else:
            came_z(u, h, d, sign, 3)

    rows_at = lax.broadcasted_iota(jnp.int32, (LANES, LANES), 0)
    for t in range(ntgt):
        a = jnp.minimum(chunks[t] - first, nwin - 2)
        want = rows_at + (col_base + t * LANES)
        table = jnp.concatenate(
            [
                jnp.where(places[pl.ds(first + a + i, 1), :] == want, 1.0, 0.0).astype(BF16)
                for i in range(2)
            ],
            axis=1,
        )
        for h in range(2):
            rows = jnp.concatenate(
                [wind[h, :, a + i].reshape(LANES, LANES) for i in range(2)], axis=0
            )
            spread[pl.ds(t * LANES, LANES), pl.ds(h * LANES, LANES)] = jnp.dot(
                table, rows, preferred_element_type=F32
            ).astype(BF16)

    given = spread.at[pl.ds(pl.multiple_of(z * own, GROUP), own)]
    give = pltpu.make_async_remote_copy(
        src_ref=given, dst_ref=own_s, send_sem=loc.at[3], recv_sem=rs,
        device_id=to_dev, device_id_type=MESH_ID,
    )

    @pl.when(goes)
    def _():
        give.start()

    @pl.when(stays)
    def _():
        copy = pltpu.make_async_copy(given, own_s, loc.at[4])
        copy.start()
        copy.wait()

    def post(value, out, dst, at, sem, device, sems):
        top = jnp.maximum(jnp.max(jnp.abs(value), axis=0, keepdims=True), TINY)
        out[...] = jnp.round(value * (LEVELS / top)).astype(jnp.int32).astype(jnp.int16)
        scale[(0, *at)] = top * (1.0 / LEVELS)
        put(scale.at[(0, *at)], scale.at[(1, *at)], sems[1], sem[1], **device)
        put(out, dst, sems[0], sem[0], **device)

    def value_of(dst, at):
        return dst[...].astype(jnp.int32).astype(F32) * scale[(1, *at)]

    def post_1(value, h, d, at, sem):
        post(value, out_1.at[h, d, at], ring_1.at[h, d, at], (0, h, d, at),
             (r1.at[0, h, sem], r1.at[1, h, sem]), step(order[h][0], 1 - 2 * d), (3, 4))

    def fetch_far(h, j):
        d, at = j // 2, SIDE + j % 2
        arrive(scale.at[1, 0, h, d, at], r1.at[1, h, SIDE + j])
        arrive(ring_1.at[h, d, at], r1.at[0, h, SIDE + j])
        return value_of(ring_1.at[h, d, at], (0, h, d, at))

    def fetch_near(h, j):
        arrive(scale.at[1, 0, h, :, j], r1.at[1, h, j])
        arrive(ring_1.at[h, :, j], r1.at[0, h, j])
        return [value_of(ring_1.at[h, d, j], (0, h, d, j)) for d in range(2)]

    def near(h, d, j):
        post_1(part[h, 1 if d == 0 else 3, j], h, d, j, j)

    def far(h, d, j):
        post_1(part[h, 2, j], h, d, SIDE + j % 2, SIDE + j)

    load_front.wait()

    def rows_of(dx, dy):
        at = (lax.rem(px + dx, SIDE) * SIDE + lax.rem(py + dy, SIDE)) * own
        return front_v[pl.ds(pl.multiple_of(at, GROUP), own), :]

    def multiply(*blocks):
        rows = jnp.concatenate([rows_of(*block) for block in blocks], axis=0)
        whole = jnp.dot(rows, spread[...], preferred_element_type=F32)
        for n, (dx, dy) in enumerate(blocks):
            part[0, dx, dy] = whole[n * own:(n + 1) * own, :LANES]
            part[1, dy, dx] = whole[n * own:(n + 1) * own, LANES:]

    multiply((2, 2))
    for h in range(2):
        far(h, 1, 2)
    multiply((2, 1), (1, 2), (2, 3), (3, 2))
    for j in (1, 3):
        for h in range(2):
            far(h, j // 2, j)
    for h in range(2):
        near(h, 0, 2)
    multiply((2, 0), (0, 2), (1, 3), (3, 1))
    for h in range(2):
        far(h, 0, 0)
    for h in range(2):
        near(h, 1, 1)
        near(h, 0, 3)
    multiply((3, 0), (0, 3))
    for h in range(2):
        near(h, 1, 0)
    multiply((3, 3), (1, 1), (1, 0), (0, 1), (0, 0))
    for j in (2, 1, 3, 0):
        for h in range(2):
            d = j // 2
            post_1(part[h, 1 if d == 0 else 3, j] + fetch_far(h, j), h, d, j, j)

    for j in (2, 1, 3, 0):
        for h in range(2):
            ahead, behind = fetch_near(h, j)
            both = part[h, 0, j] + ahead + behind
            if j:
                post(both, out_2.at[h, j - 1], ring_2.at[h, j - 1], (1, h, 0, j - 1),
                     (r2.at[0, h], r2.at[1, h]), step(order[h][1], j), (5, 6))
            else:
                mid[h] = both
    halves = []
    for h in range(2):
        arrive(scale.at[1, 1, h, 0, pl.ds(0, SIDE - 1)], r2.at[1, h])
        arrive(ring_2.at[h], r2.at[0, h])
        both = mid[h]
        for j in (1, 3, 2):
            both += value_of(ring_2.at[h, j - 1], (1, h, 0, j - 1))
        halves.append(both)
    hit_rows = hits[0]
    for h in range(2):
        off_out[:, pl.ds(h * LANES, LANES)] = jnp.where(hit_rows > 0.5, -halves[h], 0.0)
    product = jnp.concatenate(halves, axis=1)

    @pl.when(goes)
    def _():
        give.wait()

    high = product.astype(BF16)
    low = (product - high.astype(F32)).astype(BF16)
    rows = own_s[...]
    dims = (((0,), (0,)), ((), ()))
    here = lax.dot_general(rows, high, dims, preferred_element_type=F32)
    here += lax.dot_general(rows, low, dims, preferred_element_type=F32)

    def code(value):
        top = jnp.maximum(jnp.max(jnp.abs(value), axis=-2, keepdims=True), TINY)
        levels = jnp.round(value * (LEVELS / top)).astype(jnp.int32).astype(jnp.int16)
        return levels, top * (1.0 / LEVELS)

    def plain(levels, unit):
        return levels.astype(jnp.int32).astype(F32) * unit

    here = here.reshape(terms.shape)
    terms[...], dscale[0] = code(here)
    for off in others:
        peer, device = in_plane(off)
        put(dscale.at[0, peer], dscale.at[1, off - 1], 8, rd.at[1], **device)
        put(terms.at[peer], got_d.at[off - 1], 7, rd.at[0], **device)
    acc = plain(terms[col], dscale[0, col])
    arrive(dscale.at[1, pl.ds(0, SIDE * SIDE - 1)], rd.at[1])
    arrive(got_d, rd.at[0])
    for off in others:
        acc += plain(got_d[off - 1], dscale[1, off - 1])
    got_z[SPAN - 1], dscale[2, SPAN - 1] = code(acc)
    for off in planes:
        peer = lax.rem(z + off, SPAN)
        put(dscale.at[2, SPAN - 1], dscale.at[2, off - 1], 10, rzz.at[1], row=peer)
        put(got_z.at[SPAN - 1], got_z.at[off - 1], 9, rzz.at[0], row=peer)
    arrive(dscale.at[2, pl.ds(0, SPAN - 1)], rzz.at[1])
    arrive(got_z.at[pl.ds(0, SPAN - 1)], rzz.at[0])
    acc = jnp.zeros_like(acc)
    for r in range(SPAN):
        at = lax.rem(z - r + SPAN - 1 + SPAN, SPAN)
        acc += plain(got_z[at], dscale[2, at])
    total[col], dscale[3, col] = code(acc)
    for off in others:
        peer, device = in_plane(off)
        put(dscale.at[3, col], dscale.at[3, col], 12, rt.at[1], **device)
        put(total.at[col], total.at[col], 11, rt.at[0], **device)
    arrive(dscale.at[3, pl.ds(0, SIDE * SIDE - 1)], rt.at[1])
    arrive(total.at[pl.ds(0, SIDE * SIDE - 1)], rt.at[0])
    load_dinv.wait()
    diag_out[...] = dinv[...] + plain(total[...], dscale[3]).reshape(dinv.shape)
    sent(gath.at[:, pl.ds(0, (SIDE * SIDE - 1) * nblk)], 0)
    for u in range(2):
        sent(gath.at[:, pl.ds(0, (SPAN - 1) * cuts[u][1])], 1 + u)
    sent(out_1, 3)
    sent(scale.at[0, 0], 4)
    sent(out_2, 5)
    sent(scale.at[0, 1, :, 0, pl.ds(0, SIDE - 1)], 6)
    sent(got_d, 7)
    sent(dscale.at[1, pl.ds(0, SIDE * SIDE - 1)], 8)
    sent(got_z.at[pl.ds(0, SPAN - 1)], 9)
    sent(dscale.at[2, pl.ds(0, SPAN - 1)], 10)
    sent(dscale.at[3, pl.ds(0, SIDE * SIDE - 1)], 12)
    sent(total.at[pl.ds(0, SIDE * SIDE - 1)], 11)


def finish(off, diag, off_out, diag_out, sems):
    copies = [
        pltpu.make_async_copy(off, off_out, sems.at[0]),
        pltpu.make_async_copy(diag, diag_out, sems.at[1]),
    ]
    for copy in copies:
        copy.start()
    for copy in copies:
        copy.wait()


def shards(front_inverse, panel, row_map, diag_inverse):
    front_rows, front_cols = front_inverse.shape
    _, block, width = panel.shape
    count = row_map.shape[1]
    nchunk = count // LANES
    nwin = front_cols // LANES + 1
    own = front_rows // (SIDE * SIDE)
    nown = (own + 2 * LANES - 2) // LANES
    slab = width // (SIDE * SIDE)
    vmem = pltpu.VMEM
    dma = pltpu.SemaphoreType.DMA
    offdiag, diag = pl.pallas_call(
        kernel,
        out_shape=(
            jax.ShapeDtypeStruct((own, width), F32),
            jax.ShapeDtypeStruct((width, width), F32),
        ),
        in_specs=[pl.BlockSpec(memory_space=pltpu.HBM)] * 4,
        out_specs=(pl.BlockSpec(memory_space=pltpu.VMEM),) * 2,
        scratch_shapes=[
            vmem((nchunk, LANES), jnp.int32),
            vmem((width, width), F32),
            vmem((2, nchunk, GROUP, LANES), BF16),
            vmem((2, SPAN, nwin, GROUP, LANES), BF16),
            vmem((front_cols, width), BF16),
            vmem((front_rows, front_cols), BF16),
            vmem((2, SIDE, SIDE, own, LANES), F32),
            vmem((2, 2, SIDE + 2, own, LANES), jnp.int16),
            vmem((2, 2, SIDE + 2, own, LANES), jnp.int16),
            vmem((2, own, LANES), F32),
            vmem((2, SIDE - 1, own, LANES), jnp.int16),
            vmem((2, SIDE - 1, own, LANES), jnp.int16),
            vmem((2, 2, 2, 2, SIDE + 2, 1, LANES), F32),
            vmem((own, width), BF16),
            vmem((nown, own, LANES), F32),
            vmem((SIDE * SIDE, slab, width), jnp.int16),
            vmem((SIDE * SIDE - 1, slab, width), jnp.int16),
            vmem((SPAN, slab, width), jnp.int16),
            vmem((SIDE * SIDE, slab, width), jnp.int16),
            vmem((4, SIDE * SIDE, 1, width), F32),
            dma((13,)),
            dma((2, SIDE)),
            dma((2, 2, 2, SPAN // 2)),
            dma((2, 2, 2 * SIDE)),
            dma((2, 2)),
            dma,
            dma((2,)),
            dma((2,)),
            dma((2,)),
            dma((7,)),
        ],
        compiler_params=pltpu.CompilerParams(
            collective_id=0, has_side_effects=True, vmem_limit_bytes=32 * 1024 * 1024
        ),
        name="selected_inverse",
    )(
        *(
            pltpu.with_memory_space_constraint(x, pltpu.HBM)
            for x in (
                panel.reshape(block // (SPAN * GROUP), SPAN, GROUP, width),
                row_map.reshape(nchunk, LANES),
                front_inverse,
                diag_inverse[0],
            )
        )
    )
    whole = pl.BlockSpec(memory_space=pl.ANY)
    offdiag, diag = pl.pallas_call(
        finish,
        out_shape=(
            jax.ShapeDtypeStruct((own, width), F32),
            jax.ShapeDtypeStruct((width, width), F32),
        ),
        in_specs=[whole, whole],
        out_specs=(whole, whole),
        scratch_shapes=[dma((2,))],
        name="outputs",
    )(*(pltpu.with_memory_space_constraint(x, pltpu.VMEM) for x in (offdiag, diag)))
    return offdiag[None], diag[None]


def solution(mesh):
    finer = Mesh(
        mesh.devices.reshape(mesh.shape["sib"], mesh.shape["row"], SIDE, SIDE),
        ("sib", "row", "col_0", "col_1"),
    )
    return jax.shard_map(
        shards,
        mesh=finer,
        in_specs=(P("row", COL), P("sib", COL, None), P("sib", None), P("sib", None, None)),
        out_specs=(P("sib", ROW_COL, None), P("sib", None, None)),
        check_vma=False,
    )
```

```python
import functools

import jax
import jax.numpy as jnp
from jax import lax
from jax.experimental import pallas as pl
from jax.experimental.pallas import tpu as pltpu
from jax.sharding import Mesh
from jax.sharding import PartitionSpec as P

COL = ("col_0", "col_1")
ROW_COL = ("row", "col_0", "col_1")
MESH_ID = pl.DeviceIdType.MESH
LANES = 128
GROUP = 16
LEVELS = 32767.0
TINY = 1e-33
SIDE = 4
SPAN = 8
F32 = jnp.float32
BF16 = jnp.bfloat16


def kernel(
    panel, places_in, front, dinv_in, off_out, diag_out,
    places, dinv, gath, wind, spread, front_v, part, out_1, ring_1, mid, out_2, ring_2, scale, own_s, hits,
    terms, got_d, got_z, total, dscale,
    send, rg, rz, r1, r2, rs, rd, rzz, rt, loc,
):
    nblk = panel.shape[0]
    nchunk = places.shape[0]
    front_rows, front_cols = front.shape
    ntgt = front_cols // LANES
    nwin = wind.shape[2]
    own = own_s.shape[0]
    z = lax.axis_index("row")
    pos = {"col_0": lax.axis_index("col_0"), "col_1": lax.axis_index("col_1")}
    px, py = pos["col_0"], pos["col_1"]
    col = px * SIDE + py
    order = (("col_0", "col_1"), ("col_1", "col_0"))
    def put(src, dst, out, sem, **device):
        pltpu.make_async_remote_copy(
            src_ref=src, dst_ref=dst, send_sem=send.at[out], recv_sem=sem,
            device_id=device, device_id_type=MESH_ID,
        ).start()

    def arrive(dst, sem):
        pltpu.make_async_copy(dst, dst, sem).wait()

    def sent(same_bytes, out):
        pltpu.make_async_copy(same_bytes, same_bytes, send.at[out]).wait()

    def step(axis, delta):
        return {axis: lax.rem(pos[axis] + delta + SIDE, SIDE)}

    def in_plane(off):
        x, y = lax.rem(px + off // SIDE, SIDE), lax.rem(py + off % SIDE, SIDE)
        return x * SIDE + y, {"col_0": x, "col_1": y}

    others = (10, 6, 14, 9, 11, 2, 8, 5, 7, 13, 15, 1, 3, 4, 12)
    planes = (4, 3, 5, 2, 6, 1, 7)

    to_row = col // 2
    to_col = SPAN * lax.rem(col, 2) + z
    from_col = 2 * z + col // SPAN
    from_row = lax.rem(col, SPAN)
    stays = jnp.logical_and(to_row == z, to_col == col)
    goes = jnp.logical_not(stays)
    to_dev = {"row": to_row, "col_0": to_col // SIDE, "col_1": lax.rem(to_col, SIDE)}
    from_dev = {"row": from_row, "col_0": from_col // SIDE, "col_1": lax.rem(from_col, SIDE)}

    load_front = pltpu.make_async_copy(front, front_v, loc.at[0])
    load_front.start()
    load_places = pltpu.make_async_copy(places_in, places, loc.at[5])
    load_places.start()
    load_dinv = pltpu.make_async_copy(dinv_in, dinv, loc.at[6])
    load_dinv.start()

    barrier = pltpu.get_barrier_semaphore()
    for axis in ("col_0", "col_1"):
        for delta in (1, -1, 2):
            pl.semaphore_signal(
                barrier, inc=1, device_id=step(axis, delta), device_id_type=MESH_ID
            )
    for delta in (2, -2, 1, -1):
        pl.semaphore_signal(
            barrier, inc=1, device_id={"row": lax.rem(z + delta + SPAN, SPAN)},
            device_id_type=MESH_ID,
        )
    pl.semaphore_wait(barrier, 2 * (SIDE - 1) + 4)

    def slot(h, d0, d1):
        a0, a1 = order[h]
        c0 = lax.rem(pos[a0] + d0, SIDE)
        c1 = lax.rem(pos[a1] + d1, SIDE)
        k = c0 * SIDE + c1 if h == 0 else c1 * SIDE + c0
        return gath.at[h, pl.ds(k * nblk, nblk)]

    def mine(h):
        return panel.at[:, z, :, pl.ds(h * LANES, LANES)]

    def pass_on(h, d0, d1, which, delta, src=None):
        dst = slot(h, d0, d1)
        sem = rg.at[h, 0 if which else (d0 - delta) % SIDE]
        put(dst if src is None else src, dst, 0, sem, **step(order[h][which], delta))

    def gathered(h, d0):
        arrive(slot(h, d0, 0), rg.at[h, d0])

    for h in range(2):
        for delta in (2, 1, -1):
            pass_on(h, 0, 0, 0, delta, mine(h))
    for h in range(2):
        for delta in (2, 1, -1):
            pass_on(h, 0, 0, 1, delta, mine(h))
    keep = [pltpu.make_async_copy(mine(h), slot(h, 0, 0), loc.at[1 + h]) for h in range(2)]
    for copy in keep:
        copy.start()

    load_places.wait()
    place = places[...]

    def chunk_of(bound):
        return jnp.sum((place < bound).astype(jnp.int32)) // LANES

    col_base = col * front_cols
    chunks = [chunk_of(col_base + t * LANES) for t in range(ntgt)]
    first = jnp.minimum(chunks[0], nchunk - nwin)
    own_base = z * front_rows + col * own
    nown = hits.shape[0]
    own_first = jnp.minimum(chunk_of(own_base), nchunk - nown)
    target = lax.broadcasted_iota(jnp.int32, (own, LANES), 0) + own_base
    mark = jnp.zeros((own, LANES), F32)
    for i in range(nown):
        mark += jnp.where(places[pl.ds(own_first + i, 1), :] == target, 1.0, 0.0)
    hit_rows = jnp.broadcast_to(jnp.max(mark, axis=1, keepdims=True), (own, LANES))
    hits[0] = hit_rows

    for d in (1, 3, 2):
        for h in range(2):
            gathered(h, d)
            for delta in (2, 1, -1):
                pass_on(h, d, 0, 1, delta)
    for copy in keep:
        copy.wait()
    for h in range(2):
        arrive(gath.at[h, pl.ds(0, SIDE * (SIDE - 1) * nblk)], rg.at[h, 0])

    for h in range(2):
        for i in range(nwin):
            wind[h, z, i] = gath[h, first + i]

    cuts = ((0, nwin // 2), (nwin // 2, nwin - nwin // 2))

    def share(h, u, d):
        return wind.at[h, lax.rem(z + d + SPAN, SPAN), pl.ds(*cuts[u])]

    pieces = [(u, h, d, 1 - 2 * d) for u in range(2) for h in range(2) for d in range(2)]

    def pass_z(u, h, d, sign, origin, hops):
        block = share(h, u, -sign * origin)
        put(block, block, 1 + u, rz.at[h, u, d, origin + hops - 1],
            row=lax.rem(z + sign * hops + SPAN, SPAN))

    def came_z(u, h, d, sign, origin):
        arrive(share(h, u, -sign * origin), rz.at[h, u, d, origin - 1])

    for u, h, d, sign in pieces:
        if h != d:
            pass_z(u, h, d, sign, 0, 1)
    for u, h, d, sign in pieces:
        if h == d:
            pass_z(u, h, d, sign, 0, 2)
    for u, h, d, sign in pieces:
        if h == d:
            pass_z(u, h, d, sign, 0, 1)
    for u, h, d, sign in pieces:
        if h != d:
            came_z(u, h, d, sign, 1)
            pass_z(u, h, d, sign, 1, 1)
    for u, h, d, sign in pieces:
        if h == d:
            came_z(u, h, d, sign, 2)
            pass_z(u, h, d, sign, 2, 2)
    for u, h, d, sign in pieces:
        if h == d:
            pass_z(u, h, d, sign, 2, 1)
    for u, h, d, sign in pieces:
        if h != d:
            came_z(u, h, d, sign, 2)
            pass_z(u, h, d, sign, 2, 1)
    for u, h, d, sign in pieces:
        if h == d:
            came_z(u, h, d, sign, 1)
            came_z(u, h, d, sign, 3)
            came_z(u, h, d, sign, 4)
        else:
            came_z(u, h, d, sign, 3)

    rows_at = lax.broadcasted_iota(jnp.int32, (LANES, LANES), 0)
    for t in range(ntgt):
        a = jnp.minimum(chunks[t] - first, nwin - 2)
        want = rows_at + (col_base + t * LANES)
        table = jnp.concatenate(
            [
                jnp.where(places[pl.ds(first + a + i, 1), :] == want, 1.0, 0.0).astype(BF16)
                for i in range(2)
            ],
            axis=1,
        )
        for h in range(2):
            rows = jnp.concatenate(
                [wind[h, :, a + i].reshape(LANES, LANES) for i in range(2)], axis=0
            )
            spread[pl.ds(t * LANES, LANES), pl.ds(h * LANES, LANES)] = jnp.dot(
                table, rows, preferred_element_type=F32
            ).astype(BF16)

    given = spread.at[pl.ds(pl.multiple_of(z * own, GROUP), own)]
    give = pltpu.make_async_remote_copy(
        src_ref=given, dst_ref=own_s, send_sem=loc.at[3], recv_sem=rs,
        device_id=to_dev, device_id_type=MESH_ID,
    )

    @pl.when(goes)
    def _():
        give.start()

    @pl.when(stays)
    def _():
        copy = pltpu.make_async_copy(given, own_s, loc.at[4])
        copy.start()
        copy.wait()

    def post(value, out, dst, at, sem, device, sems):
        top = jnp.maximum(jnp.max(jnp.abs(value), axis=0, keepdims=True), TINY)
        out[...] = jnp.round(value * (LEVELS / top)).astype(jnp.int32).astype(jnp.int16)
        scale[(0, *at)] = top * (1.0 / LEVELS)
        put(scale.at[(0, *at)], scale.at[(1, *at)], sems[1], sem[1], **device)
        put(out, dst, sems[0], sem[0], **device)

    def value_of(dst, at):
        return dst[...].astype(jnp.int32).astype(F32) * scale[(1, *at)]

    def post_1(value, h, d, at, sem):
        post(value, out_1.at[h, d, at], ring_1.at[h, d, at], (0, h, d, at),
             (r1.at[0, h, sem], r1.at[1, h, sem]), step(order[h][0], 1 - 2 * d), (3, 4))

    def fetch_far(h, j):
        d, at = j // 2, SIDE + j % 2
        arrive(scale.at[1, 0, h, d, at], r1.at[1, h, SIDE + j])
        arrive(ring_1.at[h, d, at], r1.at[0, h, SIDE + j])
        return value_of(ring_1.at[h, d, at], (0, h, d, at))

    def fetch_near(h, j):
        arrive(scale.at[1, 0, h, :, j], r1.at[1, h, j])
        arrive(ring_1.at[h, :, j], r1.at[0, h, j])
        return [value_of(ring_1.at[h, d, j], (0, h, d, j)) for d in range(2)]

    def near(h, d, j):
        post_1(part[h, 1 if d == 0 else 3, j], h, d, j, j)

    def far(h, d, j):
        post_1(part[h, 2, j], h, d, SIDE + j % 2, SIDE + j)

    load_front.wait()

    def rows_of(dx, dy):
        at = (lax.rem(px + dx, SIDE) * SIDE + lax.rem(py + dy, SIDE)) * own
        return front_v[pl.ds(pl.multiple_of(at, GROUP), own), :]

    def multiply(*blocks):
        rows = jnp.concatenate([rows_of(*block) for block in blocks], axis=0)
        whole = jnp.dot(rows, spread[...], preferred_element_type=F32)
        for n, (dx, dy) in enumerate(blocks):
            part[0, dx, dy] = whole[n * own:(n + 1) * own, :LANES]
            part[1, dy, dx] = whole[n * own:(n + 1) * own, LANES:]

    multiply((2, 2))
    for h in range(2):
        far(h, 1, 2)
    multiply((2, 1), (1, 2))
    for h in range(2):
        far(h, 0, 1)
    multiply((2, 3), (3, 2))
    for h in range(2):
        far(h, 1, 3)
    for h in range(2):
        near(h, 0, 2)
    multiply((2, 0), (0, 2), (1, 3), (3, 1))
    for h in range(2):
        far(h, 0, 0)
    for h in range(2):
        near(h, 1, 1)
        near(h, 0, 3)
    multiply((3, 0), (0, 3))
    for h in range(2):
        near(h, 1, 0)
    multiply((3, 3), (1, 1), (1, 0), (0, 1), (0, 0))
    for j in (2, 1, 3, 0):
        for h in range(2):
            d = j // 2
            post_1(part[h, 1 if d == 0 else 3, j] + fetch_far(h, j), h, d, j, j)

    for j in (2, 1, 3, 0):
        for h in range(2):
            ahead, behind = fetch_near(h, j)
            both = part[h, 0, j] + ahead + behind
            if j:
                post(both, out_2.at[h, j - 1], ring_2.at[h, j - 1], (1, h, 0, j - 1),
                     (r2.at[0, h], r2.at[1, h]), step(order[h][1], j), (5, 6))
            else:
                mid[h] = both
    halves = []
    for h in range(2):
        arrive(scale.at[1, 1, h, 0, pl.ds(0, SIDE - 1)], r2.at[1, h])
        arrive(ring_2.at[h], r2.at[0, h])
        both = mid[h]
        for j in (1, 3, 2):
            both += value_of(ring_2.at[h, j - 1], (1, h, 0, j - 1))
        halves.append(both)
    hit_rows = hits[0]
    for h in range(2):
        off_out[:, pl.ds(h * LANES, LANES)] = jnp.where(hit_rows > 0.5, -halves[h], 0.0)
    product = jnp.concatenate(halves, axis=1)

    @pl.when(goes)
    def _():
        give.wait()

    high = product.astype(BF16)
    low = (product - high.astype(F32)).astype(BF16)
    rows = own_s[...]
    dims = (((0,), (0,)), ((), ()))
    here = lax.dot_general(rows, high, dims, preferred_element_type=F32)
    here += lax.dot_general(rows, low, dims, preferred_element_type=F32)

    def code(value):
        top = jnp.maximum(jnp.max(jnp.abs(value), axis=-2, keepdims=True), TINY)
        levels = jnp.round(value * (LEVELS / top)).astype(jnp.int32).astype(jnp.int16)
        return levels, top * (1.0 / LEVELS)

    def plain(levels, unit):
        return levels.astype(jnp.int32).astype(F32) * unit

    here = here.reshape(terms.shape)
    terms[...], dscale[0] = code(here)
    for off in others:
        peer, device = in_plane(off)
        put(dscale.at[0, peer], dscale.at[1, off - 1], 8, rd.at[1], **device)
        put(terms.at[peer], got_d.at[off - 1], 7, rd.at[0], **device)
    acc = plain(terms[col], dscale[0, col])
    arrive(dscale.at[1, pl.ds(0, SIDE * SIDE - 1)], rd.at[1])
    arrive(got_d, rd.at[0])
    for off in others:
        acc += plain(got_d[off - 1], dscale[1, off - 1])
    got_z[SPAN - 1], dscale[2, SPAN - 1] = code(acc)
    for off in planes:
        peer = lax.rem(z + off, SPAN)
        put(dscale.at[2, SPAN - 1], dscale.at[2, off - 1], 10, rzz.at[1], row=peer)
        put(got_z.at[SPAN - 1], got_z.at[off - 1], 9, rzz.at[0], row=peer)
    arrive(dscale.at[2, pl.ds(0, SPAN - 1)], rzz.at[1])
    arrive(got_z.at[pl.ds(0, SPAN - 1)], rzz.at[0])
    acc = jnp.zeros_like(acc)
    for r in range(SPAN):
        at = lax.rem(z - r + SPAN - 1 + SPAN, SPAN)
        acc += plain(got_z[at], dscale[2, at])
    total[col], dscale[3, col] = code(acc)
    for off in others:
        peer, device = in_plane(off)
        put(dscale.at[3, col], dscale.at[3, col], 12, rt.at[1], **device)
        put(total.at[col], total.at[col], 11, rt.at[0], **device)
    arrive(dscale.at[3, pl.ds(0, SIDE * SIDE - 1)], rt.at[1])
    arrive(total.at[pl.ds(0, SIDE * SIDE - 1)], rt.at[0])
    load_dinv.wait()
    diag_out[...] = dinv[...] + plain(total[...], dscale[3]).reshape(dinv.shape)
    sent(gath.at[:, pl.ds(0, (SIDE * SIDE - 1) * nblk)], 0)
    for u in range(2):
        sent(gath.at[:, pl.ds(0, (SPAN - 1) * cuts[u][1])], 1 + u)
    sent(out_1, 3)
    sent(scale.at[0, 0], 4)
    sent(out_2, 5)
    sent(scale.at[0, 1, :, 0, pl.ds(0, SIDE - 1)], 6)
    sent(got_d, 7)
    sent(dscale.at[1, pl.ds(0, SIDE * SIDE - 1)], 8)
    sent(got_z.at[pl.ds(0, SPAN - 1)], 9)
    sent(dscale.at[2, pl.ds(0, SPAN - 1)], 10)
    sent(dscale.at[3, pl.ds(0, SIDE * SIDE - 1)], 12)
    sent(total.at[pl.ds(0, SIDE * SIDE - 1)], 11)


def finish(off, diag, off_out, diag_out, sems):
    copies = [
        pltpu.make_async_copy(off, off_out, sems.at[0]),
        pltpu.make_async_copy(diag, diag_out, sems.at[1]),
    ]
    for copy in copies:
        copy.start()
    for copy in copies:
        copy.wait()


def shards(front_inverse, panel, row_map, diag_inverse):
    front_rows, front_cols = front_inverse.shape
    _, block, width = panel.shape
    count = row_map.shape[1]
    nchunk = count // LANES
    nwin = front_cols // LANES + 1
    own = front_rows // (SIDE * SIDE)
    nown = (own + 2 * LANES - 2) // LANES
    slab = width // (SIDE * SIDE)
    vmem = pltpu.VMEM
    dma = pltpu.SemaphoreType.DMA
    offdiag, diag = pl.pallas_call(
        kernel,
        out_shape=(
            jax.ShapeDtypeStruct((own, width), F32),
            jax.ShapeDtypeStruct((width, width), F32),
        ),
        in_specs=[pl.BlockSpec(memory_space=pltpu.HBM)] * 4,
        out_specs=(pl.BlockSpec(memory_space=pltpu.VMEM),) * 2,
        scratch_shapes=[
            vmem((nchunk, LANES), jnp.int32),
            vmem((width, width), F32),
            vmem((2, nchunk, GROUP, LANES), BF16),
            vmem((2, SPAN, nwin, GROUP, LANES), BF16),
            vmem((front_cols, width), BF16),
            vmem((front_rows, front_cols), BF16),
            vmem((2, SIDE, SIDE, own, LANES), F32),
            vmem((2, 2, SIDE + 2, own, LANES), jnp.int16),
            vmem((2, 2, SIDE + 2, own, LANES), jnp.int16),
            vmem((2, own, LANES), F32),
            vmem((2, SIDE - 1, own, LANES), jnp.int16),
            vmem((2, SIDE - 1, own, LANES), jnp.int16),
            vmem((2, 2, 2, 2, SIDE + 2, 1, LANES), F32),
            vmem((own, width), BF16),
            vmem((nown, own, LANES), F32),
            vmem((SIDE * SIDE, slab, width), jnp.int16),
            vmem((SIDE * SIDE - 1, slab, width), jnp.int16),
            vmem((SPAN, slab, width), jnp.int16),
            vmem((SIDE * SIDE, slab, width), jnp.int16),
            vmem((4, SIDE * SIDE, 1, width), F32),
            dma((13,)),
            dma((2, SIDE)),
            dma((2, 2, 2, SPAN // 2)),
            dma((2, 2, 2 * SIDE)),
            dma((2, 2)),
            dma,
            dma((2,)),
            dma((2,)),
            dma((2,)),
            dma((7,)),
        ],
        compiler_params=pltpu.CompilerParams(
            collective_id=0, has_side_effects=True, vmem_limit_bytes=32 * 1024 * 1024
        ),
        name="selected_inverse",
    )(
        *(
            pltpu.with_memory_space_constraint(x, pltpu.HBM)
            for x in (
                panel.reshape(block // (SPAN * GROUP), SPAN, GROUP, width),
                row_map.reshape(nchunk, LANES),
                front_inverse,
                diag_inverse[0],
            )
        )
    )
    whole = pl.BlockSpec(memory_space=pl.ANY)
    offdiag, diag = pl.pallas_call(
        finish,
        out_shape=(
            jax.ShapeDtypeStruct((own, width), F32),
            jax.ShapeDtypeStruct((width, width), F32),
        ),
        in_specs=[whole, whole],
        out_specs=(whole, whole),
        scratch_shapes=[dma((2,))],
        name="outputs",
    )(*(pltpu.with_memory_space_constraint(x, pltpu.VMEM) for x in (offdiag, diag)))
    return offdiag[None], diag[None]


def solution(mesh):
    finer = Mesh(
        mesh.devices.reshape(mesh.shape["sib"], mesh.shape["row"], SIDE, SIDE),
        ("sib", "row", "col_0", "col_1"),
    )
    return jax.shard_map(
        shards,
        mesh=finer,
        in_specs=(P("row", COL), P("sib", COL, None), P("sib", None), P("sib", None, None)),
        out_specs=(P("sib", ROW_COL, None), P("sib", None, None)),
        check_vma=False,
    )
```
